256 devices in a mesh: req: 64 (over z, y, core), ad: 4 (over x).
Axes of the slice: x: 4, y: 4, z: 8, core: 2. Of those that a mesh axis runs over, the one named last changes fastest.
Arguments:
- layer_input_hidden: bfloat16 [229376, 1536], P(('req', 'ad')), may hold values from -6 to 6
- input_norm_scale: float32 [1536], replicated, may hold values from 0.25 to 1.75
- query_key_value_weight: bfloat16 [1536, 3072], P(None, 'ad')
- output_weight: bfloat16 [1536, 1536], replicated, may hold values from -0.15625 to 0.15625
- adapter_down_weight: bfloat16 [64, 32, 1536], P('req'), may hold values from -0.15625 to 0.15625
- adapter_up_weight: bfloat16 [64, 16, 2304], P('req'), may hold values from -1.5 to 1.5
- prompt_token_length: int32 [256, 64], P(('req', 'ad')), may hold values from 12 to 16, as said below
- request_adapter_index: int32 [256, 64], P(('req', 'ad')), may hold values from 0 to 63, as said below
- adapter_holder_index: int32 [64], replicated, may hold values from 0 to 63, each once
Outputs:
- mixed: bfloat16 [229376, 1536], P(('req', 'ad'))
The draws below stay inside these ranges and needn't reach their ends.
Inputs may be any that keep to these rules, and one draw needn't show every extreme that they name: `prompt_token_length`: requests 2i and 2i + 1 of one device hold 28 tokens together; request j has 16 tokens wherever j is a multiple of 64. `request_adapter_index`: on one device, requests j and k name the same adapter exactly when j - k is a multiple of 64; every request j that is a multiple of 64 names one adapter, the same on all devices. So one device's tokens naming one adapter number at most 16, and exactly 16 for that common adapter.
All inputs are finite; a program needn't handle non-finite values.
Results may differ from the reference program's by a relative error of at most 0.012.
Values may be sent and summed in bfloat16 or wider, within the bound.
A program may use at most 128 MiB of HBM per device.

```python
import math
import jax
import jax.numpy as jnp
from jax import lax

MODEL_WIDTH = 1536
HEADS = 16
KV_HEADS = 8
HEAD_DIM = 96
ADAPTER_RANK = 16
MAXLEN = 16
PAIR = 28
REQ_DEV = 64
QUERY_FEATURES = 1536
KEY_FEATURES = 768
TOK_DEV = 896
TOKENS = 229376
ADAPTER_TOTAL = 64
CAP = 16
N_REQ = 64
N_AD = 4


def draw_prompt_token_length(key, part):
    row_count = N_REQ * N_AD
    pair_count = REQ_DEV // 2
    first_len = jax.random.randint(jax.random.fold_in(key, 101), (row_count, pair_count), PAIR - MAXLEN, MAXLEN + 1).astype(jnp.int32)
    pair_index = jnp.arange(pair_count, dtype=jnp.int32)
    forced = 2 * pair_index % ADAPTER_TOTAL == 0
    first_len = jnp.where(forced[None, :], MAXLEN, first_len).astype(jnp.int32)
    stacked = jnp.stack([first_len, PAIR - first_len], axis=-1)
    return stacked.reshape(row_count, REQ_DEV).astype(jnp.int32)


def draw_request_adapter_index(key, part):
    row_count = N_REQ * N_AD
    common = jax.random.randint(jax.random.fold_in(key, 202), (), 0, ADAPTER_TOTAL).astype(jnp.int32)
    raw_scores = jax.random.randint(jax.random.fold_in(key, 303), (row_count, ADAPTER_TOTAL), 0, 1 << 20).astype(jnp.int32)
    distinct = raw_scores * ADAPTER_TOTAL + jnp.arange(ADAPTER_TOTAL, dtype=jnp.int32)[None, :]
    shuffled = jnp.argsort(distinct, axis=1, stable=True).astype(jnp.int32)
    swapped = jnp.where(shuffled == common, shuffled[:, :1], shuffled)
    swapped = swapped.at[:, 0].set(common)
    column_index = jnp.arange(REQ_DEV, dtype=jnp.int32) % ADAPTER_TOTAL
    return swapped[:, column_index].astype(jnp.int32)


def draw_query_key_value_weight(key, part):
    values = jax.random.normal(jax.random.fold_in(key, 404), (MODEL_WIDTH, QUERY_FEATURES + 2 * KEY_FEATURES), jnp.float32) * MODEL_WIDTH ** (-0.5)
    return values.astype(jnp.bfloat16)


def level_of(rng, extent, split, least, top_value):
    def one(dim, shards_of):
        heights = jax.random.uniform(jax.random.fold_in(jax.random.fold_in(rng, 6), dim), (shards_of,), jnp.float32, least / len(split), top_value / len(split))
        return jnp.repeat(jnp.exp(heights), extent[dim] // shards_of).reshape((-1,) + (1,) * (len(extent) - dim - 1))

    loudness = one(*split[0])
    for cut in split[1:]:
        loudness = loudness * one(*cut)
    return loudness


def gaussian(stream_key, shape, deviation, reach, cuts=(), kind=jnp.bfloat16):
    result = jax.random.normal(stream_key, shape, jnp.float32) * deviation
    if len(cuts) > 0:
        result = level_of(stream_key, shape, cuts, -0.22, 0.18) * result
    return jnp.clip(result, min=-reach, max=reach).astype(kind)


def setup_inputs(seed: int = 0) -> dict:
    streams_of = jax.random.split(jax.random.key(seed), 10)
    return {
        "layer_input_hidden": gaussian(streams_of[0], (TOKENS, MODEL_WIDTH), 1.0, 6.0, ((0, 256),)),
        "input_norm_scale": jnp.clip(1.0 + 0.15 * jax.random.normal(streams_of[1], (MODEL_WIDTH,), jnp.float32), 0.25, 1.75),
        "query_key_value_weight": draw_query_key_value_weight(jax.random.fold_in(streams_of[9], 71), 0),
        "output_weight": gaussian(streams_of[3], (QUERY_FEATURES, MODEL_WIDTH), QUERY_FEATURES ** -0.5, 0.15625),
        "adapter_down_weight": gaussian(streams_of[4], (ADAPTER_TOTAL, 2 * ADAPTER_RANK, MODEL_WIDTH), MODEL_WIDTH ** -0.5, 0.15625, ((0, 64),)),
        "adapter_up_weight": gaussian(streams_of[5], (ADAPTER_TOTAL, ADAPTER_RANK, QUERY_FEATURES + KEY_FEATURES), ADAPTER_RANK ** -0.5, 1.5, ((0, 64),)),
        "prompt_token_length": draw_prompt_token_length(jax.random.fold_in(streams_of[9], 71), 0),
        "request_adapter_index": draw_request_adapter_index(jax.random.fold_in(streams_of[9], 71), 0),
        "adapter_holder_index": jax.random.permutation(streams_of[8], ADAPTER_TOTAL).astype(jnp.int32),
    }


rope_theta = 100000.0

def token_layout(lengths, adapters, owner, tok_count, capacity):
    req_count = lengths.shape[0]
    req_ends = jnp.cumsum(lengths).astype(jnp.int32)
    req_starts = (req_ends - lengths).astype(jnp.int32)
    tok_index = jnp.arange(tok_count, dtype=jnp.int32)
    member = (tok_index[:, None] >= req_starts[None, :]) & (tok_index[:, None] < req_ends[None, :])
    inside = (tok_index - lax.optimization_barrier(jnp.sum(jnp.where(member, req_starts[None, :], 0), axis=1))).astype(jnp.int32)
    adapter_ids = jnp.arange(owner.shape[0], dtype=jnp.int32)
    slot_req = lax.optimization_barrier(jnp.sum(jnp.where(adapters[:, None] == adapter_ids[None, :], owner[None, :], 0), axis=1)).astype(jnp.int32)
    req_order = jnp.arange(req_count, dtype=jnp.int32)
    earlier = (slot_req[:, None] == slot_req[None, :]) & (req_order[None, :] < req_order[:, None])
    offset_req = lax.optimization_barrier(jnp.sum(jnp.where(earlier, lengths[None, :], 0), axis=1)).astype(jnp.int32)
    slot_token_rows = lax.optimization_barrier(jnp.sum(jnp.where(member, slot_req[None, :], 0), axis=1)).astype(jnp.int32)
    offset_tok = lax.optimization_barrier(jnp.sum(jnp.where(member, offset_req[None, :], 0), axis=1)).astype(jnp.int32)
    request = lax.optimization_barrier(jnp.sum(jnp.where(member, req_order[None, :], 0), axis=1)).astype(jnp.int32)
    dest_row = (slot_token_rows * capacity + offset_tok + inside).astype(jnp.int32)
    return (inside, slot_token_rows, dest_row, request)

def rotate(values, position):
    half_width = values.shape[-1] // 2
    inverse_freq = jnp.exp(-math.log(rope_theta) * 2.0 * jnp.arange(half_width, dtype=jnp.float32) / values.shape[-1])
    angles = position.astype(jnp.float32)[:, None] * inverse_freq[None, :]
    cosine = jnp.cos(angles)[:, None, :]
    sine_part = jnp.sin(angles)[:, None, :]
    first_half = values[..., :half_width]
    second_half = values[..., half_width:]
    return jnp.concatenate([first_half * cosine - second_half * sine_part, second_half * cosine + first_half * sine_part], axis=-1)

def attend(query, key, value, request):
    tok_count = query.shape[0]
    pair_count = tok_count // PAIR
    group_size = HEADS // KV_HEADS
    score_scale = 1.0 / math.sqrt(HEAD_DIM)
    query_g = query.reshape(pair_count, PAIR, KV_HEADS, group_size, HEAD_DIM).transpose(2, 0, 3, 1, 4)
    key_g = key.reshape(pair_count, PAIR, KV_HEADS, HEAD_DIM).transpose(2, 0, 1, 3)
    value_g = value.reshape(pair_count, PAIR, KV_HEADS, HEAD_DIM).transpose(2, 0, 1, 3)
    req_pair = request.reshape(pair_count, PAIR)
    inner = jnp.arange(PAIR, dtype=jnp.int32)
    allowed = (req_pair[:, :, None] == req_pair[:, None, :]) & (inner[None, :] <= inner[:, None])[None]

    def head_group(operands):
        q_blk, k_blk, v_blk = operands
        scores = jnp.einsum('pgqd,pkd->pgqk', q_blk.astype(jnp.float32), k_blk.astype(jnp.float32)) * score_scale
        scores = jnp.where(allowed[:, None], scores, -jnp.inf)
        row_max = lax.optimization_barrier(jnp.max(scores, axis=-1, keepdims=True))
        weights = jnp.exp(scores - row_max)
        probs = (weights / lax.optimization_barrier(jnp.sum(weights, axis=-1, keepdims=True))).astype(jnp.bfloat16)
        return jnp.einsum('pgqk,pkd->pgqd', probs.astype(jnp.float32), v_blk.astype(jnp.float32)).astype(jnp.bfloat16)
    attended = lax.map(head_group, (query_g, key_g, value_g))
    return attended.transpose(1, 3, 0, 2, 4).reshape(tok_count, HEADS * HEAD_DIM)

def reference(layer_input_hidden, input_norm_scale, query_key_value_weight, output_weight, adapter_down_weight, adapter_up_weight, prompt_token_length, request_adapter_index, adapter_holder_index):
    query_column_width = HEADS * HEAD_DIM
    kv_width = KV_HEADS * HEAD_DIM
    block_count = prompt_token_length.shape[0]
    blocks = layer_input_hidden.reshape(block_count, TOK_DEV, MODEL_WIDTH)

    def one_block(operands):
        hidden, lengths, adapters = operands
        widened = hidden.astype(jnp.float32)
        normed = (widened * lax.rsqrt(lax.optimization_barrier(jnp.mean(widened * widened, axis=-1, keepdims=True)) + 1e-05) * input_norm_scale).astype(jnp.bfloat16)
        position, slot_token_rows, dest_row, request = token_layout(lengths, adapters, adapter_holder_index, TOK_DEV, CAP)
        projected = jnp.dot(normed, query_key_value_weight, preferred_element_type=jnp.float32)
        down_token_rows = adapter_down_weight[slot_token_rows].astype(jnp.float32)
        low_rows = jnp.einsum('td,trd->tr', normed.astype(jnp.float32), down_token_rows).astype(jnp.bfloat16)
        up_token_rows = adapter_up_weight[slot_token_rows].astype(jnp.float32)
        low_wide = low_rows.astype(jnp.float32)
        delta_q = jnp.einsum('tr,tre->te', low_wide[:, :ADAPTER_RANK], up_token_rows[:, :, :query_column_width]).astype(jnp.bfloat16)
        delta_v = jnp.einsum('tr,tre->te', low_wide[:, ADAPTER_RANK:], up_token_rows[:, :, query_column_width:]).astype(jnp.bfloat16)
        query = projected[:, :query_column_width] + delta_q.astype(jnp.float32)
        key = projected[:, query_column_width:query_column_width + kv_width]
        value = (projected[:, query_column_width + kv_width:] + delta_v.astype(jnp.float32)).astype(jnp.bfloat16)
        query = rotate(query.reshape(TOK_DEV, HEADS, HEAD_DIM), position).astype(jnp.bfloat16)
        key = rotate(key.reshape(TOK_DEV, KV_HEADS, HEAD_DIM), position).astype(jnp.bfloat16)
        value = value.reshape(TOK_DEV, KV_HEADS, HEAD_DIM)
        attended = attend(query, key, value, request)
        return (widened + jnp.dot(attended, output_weight, preferred_element_type=jnp.float32)).astype(jnp.bfloat16)
    mixed = lax.map(one_block, (blocks, prompt_token_length, request_adapter_index))
    return mixed.reshape(block_count * TOK_DEV, MODEL_WIDTH)
```

```python
import math

import jax
import jax.numpy as jnp
import ml_dtypes
import numpy as np
from jax import lax
from jax.experimental import pallas as pl
from jax.experimental.pallas import tpu as pltpu
from jax.sharding import PartitionSpec as P

D = 1536
HEADS = 16
KV_HEADS = 8
HEAD_DIM = 96
HALF = 48
PAIR = 28
RANK = 16
SHARD = 768
TOK = 896
GROUPS = 8
GTOK = 112
GREQ = 8
KPAD = 128
UPC = 2304
ROPE_THETA = 100000.0
F32 = jnp.float32
BF16 = jnp.bfloat16
NT = (((1,), (1,)), ((), ()))
SLOT_WINDOW = [(48 * s // 128, (48 * s + 47) // 128 + 1) for s in range(8)]


def source_columns(ad, dst):
    second = dst // 384
    slot = dst % 384 // 48
    feat = dst % 48
    parity = jnp.where(ad == 0, slot // 4, 1 - slot // 4)
    q_head = 2 * (slot % 4) + parity
    q_src = q_head * 96 + second * 48 + feat
    k_src = slot * 96 + second * 48 + feat
    return jnp.where(ad < 2, q_src, jnp.where(ad == 2, k_src, dst))


def permute_shard(w, ad):
    dst = lax.broadcasted_iota(jnp.int32, (SHARD, SHARD), 1)
    src = lax.broadcasted_iota(jnp.int32, (SHARD, SHARD), 0)
    onehot = (source_columns(ad, dst) == src).astype(BF16)
    return jnp.dot(w, onehot, preferred_element_type=F32).astype(BF16)


def permute_up(up):
    r = up.shape[0]
    q = up[:, :D].reshape(r, 2, 4, 2, 2, HALF)
    first = q[:, 0].transpose(0, 3, 2, 1, 4)
    other = q[:, 1].transpose(0, 3, 2, 1, 4)[:, :, ::-1]
    return jnp.concatenate([first.reshape(r, SHARD), other.reshape(r, SHARD), up[:, D:]], axis=1)


def rope_table():
    pos = np.arange(16, dtype=np.float32)[:, None]
    inv = np.exp(np.float32(-math.log(ROPE_THETA) * 2.0) * np.arange(HALF, dtype=np.float32) / np.float32(HEAD_DIM))
    ang = (pos * inv[None, :].astype(np.float32)).astype(np.float64)
    full = np.concatenate([np.tile(np.cos(ang), (1, 8)), np.tile(np.sin(ang), (1, 8))], axis=1).astype(np.float32)
    parts = []
    rest = full
    for _ in range(3):
        piece = rest.astype(ml_dtypes.bfloat16)
        parts.append(piece)
        rest = rest - piece.astype(np.float32)
    return np.concatenate(parts, axis=0)


def attend_kernel(
    len_ref, ada_ref, hold_ref, gain_ref, tab_ref,
    x_hbm, proj_hbm, down_hbm, up_hbm, wo_hbm,
    out_ref,
    x_v, proj_v, d_v, u_v, wo_v, att_v, kmask_v, vmask_v, k_v, v_v,
    sem_x, sem_p, sem_d, sem_u, sem_wo,
):
    def row_copies(g):
        rows = pl.ds(pl.multiple_of(g * GTOK, 16), GTOK)
        return (
            pltpu.make_async_copy(x_hbm.at[rows], x_v.at[rows], sem_x.at[g]),
            pltpu.make_async_copy(proj_hbm.at[rows], proj_v.at[rows], sem_p.at[g]),
        )

    def start_group(g, carry):
        for copy in row_copies(g):
            copy.start()
        for j in range(GREQ):
            owner = hold_ref[ada_ref[g * GREQ + j]]
            pltpu.make_async_copy(down_hbm.at[owner, pl.ds(0, RANK)], d_v.at[g, pl.ds(RANK * j, RANK)], sem_d.at[g]).start()
            pltpu.make_async_copy(down_hbm.at[owner, pl.ds(RANK, RANK)], d_v.at[g, pl.ds(128 + RANK * j, RANK)], sem_d.at[g]).start()
            pltpu.make_async_copy(up_hbm.at[owner], u_v.at[g, pl.ds(RANK * j, RANK)], sem_u.at[g]).start()
        return carry

    lax.fori_loop(0, GROUPS, start_group, 0)
    wo_copies = []
    for head in range(HEADS):
        kv, parity = head // 2, head % 2
        dst = (kv // 4) * 768 + parity * 384 + (kv % 4) * 96
        wo_copies.append(pltpu.make_async_copy(wo_hbm.at[pl.ds(head * 96, 96)], wo_v.at[pl.ds(dst, 96)], sem_wo))
    for copy in wo_copies:
        copy.start()

    lane = lax.broadcasted_iota(jnp.int32, (KPAD, 384), 1)
    for s in range(8):
        kmask_v[s] = jnp.where((lane >= 48 * s) & (lane < 48 * s + 48), 1.0, 0.0).astype(BF16)
    for s in range(4):
        vmask_v[s] = jnp.where((lane >= 96 * s) & (lane < 96 * s + 96), 1.0, 0.0).astype(BF16)
    k_v[pl.ds(GTOK, KPAD - GTOK), :] = jnp.zeros((KPAD - GTOK, 768), BF16)
    v_v[pl.ds(GTOK, KPAD - GTOK), :] = jnp.zeros((KPAD - GTOK, 768), BF16)

    def group(g, carry):
        rows = pl.ds(pl.multiple_of(g * GTOK, 16), GTOK)
        t = lax.broadcasted_iota(jnp.int32, (GTOK, KPAD), 0)
        pair = t // PAIR
        first = jnp.zeros((GTOK, KPAD), jnp.int32)
        for p in range(4):
            first = jnp.where(pair == p, len_ref[g * GREQ + 2 * p], first)
        second = (t - pair * PAIR) >= first
        start = pair * PAIR + jnp.where(second, first, 0)
        request = 2 * pair + second.astype(jnp.int32)
        position = t - start
        lanes = lax.broadcasted_iota(jnp.int32, (GTOK, KPAD), 1)
        bias = jnp.where((lanes >= start) & (lanes <= t), 0.0, -jnp.inf).astype(F32)
        own = (lanes // RANK == request)
        onehot = jnp.where((lanes % 16 == position) & (lanes < 48), 1.0, 0.0).astype(BF16)[:, :48]
        rot = jnp.dot(onehot, tab_ref[...], preferred_element_type=F32)
        cosine, sine = rot[:, :384], rot[:, 384:]

        for copy in row_copies(g):
            copy.wait()
        x = x_v[rows, :].astype(F32)
        inv = lax.rsqrt(jnp.mean(x * x, axis=-1, keepdims=True) + 1e-05)
        normed = (x * inv * gain_ref[...]).astype(BF16)
        pltpu.make_async_copy(d_v.at[g], d_v.at[g], sem_d.at[g]).wait()
        low = lax.dot_general(normed, d_v[g], NT, preferred_element_type=F32)
        low_q = jnp.where(own, low[:, :128], 0.0).astype(BF16)
        low_v = jnp.where(own, low[:, 128:], 0.0).astype(BF16)
        pltpu.make_async_copy(u_v.at[g], u_v.at[g], sem_u.at[g]).wait()

        def roped(first_half, second_half):
            return first_half * cosine - second_half * sine, second_half * cosine + first_half * sine

        kf, ks = roped(proj_v[rows, D : D + 384].astype(F32), proj_v[rows, D + 384 : D + 768].astype(F32))
        k_v[:GTOK, :384] = kf.astype(BF16)
        k_v[:GTOK, 384:] = ks.astype(BF16)
        delta_v = jnp.dot(low_v, u_v[g, :, D:], preferred_element_type=F32).astype(BF16)
        v_v[:GTOK, :] = (proj_v[rows, D + 768 :].astype(F32) + delta_v.astype(F32)).astype(BF16)

        scale = 1.0 / math.sqrt(HEAD_DIM)
        for half in range(2):
            base = half * SHARD
            delta = jnp.dot(low_q, u_v[g, :, base : base + SHARD], preferred_element_type=F32).astype(BF16)
            q = proj_v[rows, base : base + SHARD].astype(F32) + delta.astype(F32)
            qf, qs = roped(q[:, :384], q[:, 384:])
            qf2 = jnp.concatenate([qf.astype(BF16), pltpu.roll(qf, 192, 1).astype(BF16)], axis=0)
            qs2 = jnp.concatenate([qs.astype(BF16), pltpu.roll(qs, 192, 1).astype(BF16)], axis=0)
            probs = []
            for s in range(4):
                slot = 4 * half + s
                lo, hi = SLOT_WINDOW[slot]
                cols = slice(128 * lo, 128 * hi)
                mask = kmask_v[slot, :, cols]
                kcat = jnp.concatenate([k_v[:, cols] * mask, k_v[:, 384 + 128 * lo : 384 + 128 * hi] * mask], axis=1)
                qcat = jnp.concatenate([qf2[:, cols], qs2[:, cols]], axis=1)
                scores = lax.dot_general(qcat, kcat, NT, preferred_element_type=F32)
                halves = []
                for b in range(2):
                    sc = scores[b * GTOK : (b + 1) * GTOK] * scale + bias
                    weights = jnp.exp(sc - jnp.max(sc, axis=-1, keepdims=True))
                    halves.append((weights / jnp.sum(weights, axis=-1, keepdims=True)).astype(BF16))
                probs.append(jnp.concatenate(halves, axis=0))
            p4 = jnp.concatenate(probs, axis=1)
            vh = v_v[:, half * 384 : half * 384 + 384]
            vstack = jnp.concatenate([vh * vmask_v[s] for s in range(4)], axis=0)
            att = jnp.dot(p4, vstack, preferred_element_type=F32).astype(BF16)
            att_v[rows, base : base + 384] = att[:GTOK]
            att_v[rows, base + 384 : base + 768] = att[GTOK:]
        return carry

    lax.fori_loop(0, GROUPS, group, 0)
    for copy in wo_copies:
        copy.wait()

    def out_rows(i, carry):
        rows = pl.ds(pl.multiple_of(i * 448, 16), 448)
        for c in range(3):
            cols = slice(512 * c, 512 * c + 512)
            acc = jnp.dot(att_v[rows, :], wo_v[:, cols], preferred_element_type=F32)
            out_ref[rows, cols] = (x_v[rows, cols].astype(F32) + acc).astype(BF16)
        return carry

    lax.fori_loop(0, 2, out_rows, 0)


def attend_call(lengths, adapters, holder, gain, x, proj, down, up, wo):
    smem = pl.BlockSpec(memory_space=pltpu.SMEM)
    vmem = pl.BlockSpec(memory_space=pltpu.VMEM)
    hbm = pl.BlockSpec(memory_space=pl.ANY)
    return pl.pallas_call(
        attend_kernel,
        out_shape=jax.ShapeDtypeStruct((TOK, D), BF16),
        in_specs=[smem, smem, smem, vmem, vmem, hbm, hbm, hbm, hbm, hbm],
        out_specs=vmem,
        scratch_shapes=[
            pltpu.VMEM((TOK, D), BF16),
            pltpu.VMEM((TOK, 2 * D), BF16),
            pltpu.VMEM((GROUPS, 256, D), BF16),
            pltpu.VMEM((GROUPS, 128, UPC), BF16),
            pltpu.VMEM((D, D), BF16),
            pltpu.VMEM((TOK, D), BF16),
            pltpu.VMEM((8, KPAD, 384), BF16),
            pltpu.VMEM((4, KPAD, 384), BF16),
            pltpu.VMEM((KPAD, 768), BF16),
            pltpu.VMEM((KPAD, 768), BF16),
            pltpu.SemaphoreType.DMA((GROUPS,)),
            pltpu.SemaphoreType.DMA((GROUPS,)),
            pltpu.SemaphoreType.DMA((GROUPS,)),
            pltpu.SemaphoreType.DMA((GROUPS,)),
            pltpu.SemaphoreType.DMA,
        ],
        compiler_params=pltpu.CompilerParams(vmem_limit_bytes=60 * 1024 * 1024),
        name="attend",
    )(lengths, adapters, holder, gain.reshape(1, D), jnp.asarray(rope_table()), x, proj, down, up, wo)


def body(hidden, gain, wqkv, wo, down, up, lengths, adapters, holder):
    ad = lax.axis_index("ad")
    w_own = permute_shard(wqkv, ad)
    w_all = lax.all_gather(w_own, "ad", axis=1, tiled=True)
    up_all = lax.all_gather(permute_up(up[0]), "req", axis=0)
    down_all = lax.all_gather(down[0], "req", axis=0)
    x = hidden.astype(F32)
    normed = (x * lax.rsqrt(jnp.mean(x * x, axis=-1, keepdims=True) + 1e-05) * gain).astype(BF16)
    proj = jnp.dot(normed, w_all, preferred_element_type=F32).astype(BF16)
    return attend_call(lengths[0], adapters[0], holder, gain, hidden, proj, down_all, up_all, wo)


def solution(mesh):
    placed = (
        P(("req", "ad"), None),
        P(),
        P(None, "ad"),
        P(),
        P("req", None, None),
        P("req", None, None),
        P(("req", "ad"), None),
        P(("req", "ad"), None),
        P(),
    )
    return jax.shard_map(
        body, mesh=mesh, in_specs=placed, out_specs=P(("req", "ad"), None), check_vma=False
    )
```

```python
import math

import jax
import jax.numpy as jnp
import ml_dtypes
import numpy as np
from jax import lax
from jax.experimental import pallas as pl
from jax.experimental.pallas import tpu as pltpu
from jax.sharding import PartitionSpec as P

D = 1536
HEADS = 16
KV_HEADS = 8
HEAD_DIM = 96
HALF = 48
PAIR = 28
RANK = 16
SHARD = 768
TOK = 896
GROUPS = 8
GTOK = 112
GREQ = 8
KPAD = 128
UPC = 2304
APC = 2 * D + UPC
NZ, NY, NX = 8, 4, 4
SUBS = 4
SUBR = D // SUBS
ROPE_THETA = 100000.0
F32 = jnp.float32
BF16 = jnp.bfloat16
NT = (((1,), (1,)), ((), ()))
SLOT_WINDOW = [(48 * s // 128, (48 * s + 47) // 128 + 1) for s in range(8)]


def source_columns(ad, dst):
    second = dst // 384
    slot = dst % 384 // 48
    feat = dst % 48
    parity = jnp.where(ad == 0, slot // 4, 1 - slot // 4)
    q_head = 2 * (slot % 4) + parity
    q_src = q_head * 96 + second * 48 + feat
    k_src = slot * 96 + second * 48 + feat
    return jnp.where(ad < 2, q_src, jnp.where(ad == 2, k_src, dst))


def permute_shard(w, ad):
    dst = lax.broadcasted_iota(jnp.int32, (SHARD, SHARD), 1)
    src = lax.broadcasted_iota(jnp.int32, (SHARD, SHARD), 0)
    onehot = (source_columns(ad, dst) == src).astype(BF16)
    return jnp.einsum("kc,cha->hka", w, onehot.reshape(SHARD, 2, 384), preferred_element_type=F32).astype(BF16)


def permute_up(up):
    r = up.shape[0]
    q = up[:, :D].reshape(r, 2, 4, 2, 2, HALF)
    first = q[:, 0].transpose(0, 3, 2, 1, 4)
    other = q[:, 1].transpose(0, 3, 2, 1, 4)[:, :, ::-1]
    return jnp.concatenate([first.reshape(r, SHARD), other.reshape(r, SHARD), up[:, D:]], axis=1)


def rope_table():
    pos = np.arange(16, dtype=np.float32)[:, None]
    inv = np.exp(np.float32(-math.log(ROPE_THETA) * 2.0) * np.arange(HALF, dtype=np.float32) / np.float32(HEAD_DIM))
    ang = (pos * inv[None, :].astype(np.float32)).astype(np.float64)
    full = np.concatenate([np.tile(np.cos(ang), (1, 8)), np.tile(np.sin(ang), (1, 8))], axis=1).astype(np.float32)
    parts = []
    rest = full
    for _ in range(3):
        piece = rest.astype(ml_dtypes.bfloat16)
        parts.append(piece)
        rest = rest - piece.astype(np.float32)
    return np.concatenate(parts, axis=0)


def attend_kernel(
    len_ref, ada_ref, hold_ref, gain_ref, tab_ref,
    x_hbm, proj_hbm, adp_hbm, wo_hbm,
    out_ref,
    x_v, proj_v, d_v, u_v, wo_v, att_v, kmask_v, vmask_v, k_v, v_v,
    sem_x, sem_p, sem_d, sem_u, sem_wo,
):
    def row_copies(g):
        rows = pl.ds(pl.multiple_of(g * GTOK, 16), GTOK)
        return (
            pltpu.make_async_copy(x_hbm.at[rows], x_v.at[rows], sem_x.at[g]),
            pltpu.make_async_copy(proj_hbm.at[:, rows], proj_v.at[:, rows], sem_p.at[g]),
        )

    def start_group(g, carry):
        for copy in row_copies(g):
            copy.start()
        for j in range(GREQ):
            owner = hold_ref[ada_ref[g * GREQ + j]]
            pltpu.make_async_copy(adp_hbm.at[owner, :, pl.ds(0, D)], d_v.at[g, pl.ds(RANK * j, RANK)], sem_d.at[g]).start()
            pltpu.make_async_copy(adp_hbm.at[owner, :, pl.ds(D, D)], d_v.at[g, pl.ds(128 + RANK * j, RANK)], sem_d.at[g]).start()
            pltpu.make_async_copy(adp_hbm.at[owner, :, pl.ds(2 * D, UPC)], u_v.at[g, pl.ds(RANK * j, RANK)], sem_u.at[g]).start()
        return carry

    lax.fori_loop(0, GROUPS, start_group, 0)
    wo_copies = []
    for head in range(HEADS):
        kv, parity = head // 2, head % 2
        dst = (kv // 4) * 768 + parity * 384 + (kv % 4) * 96
        wo_copies.append(pltpu.make_async_copy(wo_hbm.at[pl.ds(head * 96, 96)], wo_v.at[pl.ds(dst, 96)], sem_wo))
    for copy in wo_copies:
        copy.start()

    lane = lax.broadcasted_iota(jnp.int32, (KPAD, 384), 1)
    for s in range(8):
        kmask_v[s] = jnp.where((lane >= 48 * s) & (lane < 48 * s + 48), 1.0, 0.0).astype(BF16)
    for s in range(4):
        vmask_v[s] = jnp.where((lane >= 96 * s) & (lane < 96 * s + 96), 1.0, 0.0).astype(BF16)
    k_v[pl.ds(GTOK, KPAD - GTOK), :] = jnp.zeros((KPAD - GTOK, 768), BF16)
    v_v[pl.ds(GTOK, KPAD - GTOK), :] = jnp.zeros((KPAD - GTOK, 768), BF16)

    def group(g, carry):
        rows = pl.ds(pl.multiple_of(g * GTOK, 16), GTOK)
        t = lax.broadcasted_iota(jnp.int32, (GTOK, KPAD), 0)
        pair = t // PAIR
        first = jnp.zeros((GTOK, KPAD), jnp.int32)
        for p in range(4):
            first = jnp.where(pair == p, len_ref[g * GREQ + 2 * p], first)
        second = (t - pair * PAIR) >= first
        start = pair * PAIR + jnp.where(second, first, 0)
        request = 2 * pair + second.astype(jnp.int32)
        position = t - start
        lanes = lax.broadcasted_iota(jnp.int32, (GTOK, KPAD), 1)
        bias = jnp.where((lanes >= start) & (lanes <= t), 0.0, -jnp.inf).astype(F32)
        own = (lanes // RANK == request)
        onehot = jnp.where((lanes % 16 == position) & (lanes < 48), 1.0, 0.0).astype(BF16)[:, :48]
        rot = jnp.dot(onehot, tab_ref[...], preferred_element_type=F32)
        cosine, sine = rot[:, :384], rot[:, 384:]

        for copy in row_copies(g):
            copy.wait()
        x = x_v[rows, :].astype(F32)
        inv = lax.rsqrt(jnp.mean(x * x, axis=-1, keepdims=True) + 1e-05)
        normed = (x * inv * gain_ref[...]).astype(BF16)
        pltpu.make_async_copy(d_v.at[g], d_v.at[g], sem_d.at[g]).wait()
        low = lax.dot_general(normed, d_v[g], NT, preferred_element_type=F32)
        low_q = jnp.where(own, low[:, :128], 0.0).astype(BF16)
        low_v = jnp.where(own, low[:, 128:], 0.0).astype(BF16)
        pltpu.make_async_copy(u_v.at[g], u_v.at[g], sem_u.at[g]).wait()

        def roped(first_half, second_half):
            return first_half * cosine - second_half * sine, second_half * cosine + first_half * sine

        kf, ks = roped(proj_v[2, rows, :384].astype(F32), proj_v[2, rows, 384:].astype(F32))
        k_v[:GTOK, :384] = kf.astype(BF16)
        k_v[:GTOK, 384:] = ks.astype(BF16)
        delta_v = jnp.dot(low_v, u_v[g, :, D:], preferred_element_type=F32).astype(BF16)
        v_v[:GTOK, :] = (proj_v[3, rows, :].astype(F32) + delta_v.astype(F32)).astype(BF16)

        scale = 1.0 / math.sqrt(HEAD_DIM)
        for half in range(2):
            base = half * SHARD
            delta = jnp.dot(low_q, u_v[g, :, base : base + SHARD], preferred_element_type=F32).astype(BF16)
            q = proj_v[half, rows, :].astype(F32) + delta.astype(F32)
            qf, qs = roped(q[:, :384], q[:, 384:])
            qf2 = jnp.concatenate([qf.astype(BF16), pltpu.roll(qf, 192, 1).astype(BF16)], axis=0)
            qs2 = jnp.concatenate([qs.astype(BF16), pltpu.roll(qs, 192, 1).astype(BF16)], axis=0)
            probs = []
            for s in range(4):
                slot = 4 * half + s
                lo, hi = SLOT_WINDOW[slot]
                cols = slice(128 * lo, 128 * hi)
                mask = kmask_v[slot, :, cols]
                kcat = jnp.concatenate([k_v[:, cols] * mask, k_v[:, 384 + 128 * lo : 384 + 128 * hi] * mask], axis=1)
                qcat = jnp.concatenate([qf2[:, cols], qs2[:, cols]], axis=1)
                scores = lax.dot_general(qcat, kcat, NT, preferred_element_type=F32)
                halves = []
                for b in range(2):
                    sc = scores[b * GTOK : (b + 1) * GTOK] * scale + bias
                    weights = jnp.exp(sc - jnp.max(sc, axis=-1, keepdims=True))
                    halves.append((weights / jnp.sum(weights, axis=-1, keepdims=True)).astype(BF16))
                probs.append(jnp.concatenate(halves, axis=0))
            p4 = jnp.concatenate(probs, axis=1)
            vh = v_v[:, half * 384 : half * 384 + 384]
            vstack = jnp.concatenate([vh * vmask_v[s] for s in range(4)], axis=0)
            att = jnp.dot(p4, vstack, preferred_element_type=F32).astype(BF16)
            att_v[rows, base : base + 384] = att[:GTOK]
            att_v[rows, base + 384 : base + 768] = att[GTOK:]
        return carry

    lax.fori_loop(0, GROUPS, group, 0)
    for copy in wo_copies:
        copy.wait()

    def out_rows(i, carry):
        rows = pl.ds(pl.multiple_of(i * 448, 16), 448)
        for c in range(3):
            cols = slice(512 * c, 512 * c + 512)
            acc = jnp.dot(att_v[rows, :], wo_v[:, cols], preferred_element_type=F32)
            out_ref[rows, cols] = (x_v[rows, cols].astype(F32) + acc).astype(BF16)
        return carry

    lax.fori_loop(0, 2, out_rows, 0)


def attend_call(lengths, adapters, holder, gain, x, proj, adp, wo):
    smem = pl.BlockSpec(memory_space=pltpu.SMEM)
    vmem = pl.BlockSpec(memory_space=pltpu.VMEM)
    hbm = pl.BlockSpec(memory_space=pl.ANY)
    return pl.pallas_call(
        attend_kernel,
        out_shape=jax.ShapeDtypeStruct((TOK, D), BF16),
        in_specs=[smem, smem, smem, vmem, vmem, hbm, hbm, hbm, hbm],
        out_specs=vmem,
        scratch_shapes=[
            pltpu.VMEM((TOK, D), BF16),
            pltpu.VMEM((4, TOK, SHARD), BF16),
            pltpu.VMEM((GROUPS, 256, D), BF16),
            pltpu.VMEM((GROUPS, 128, UPC), BF16),
            pltpu.VMEM((D, D), BF16),
            pltpu.VMEM((TOK, D), BF16),
            pltpu.VMEM((8, KPAD, 384), BF16),
            pltpu.VMEM((4, KPAD, 384), BF16),
            pltpu.VMEM((KPAD, 768), BF16),
            pltpu.VMEM((KPAD, 768), BF16),
            pltpu.SemaphoreType.DMA((GROUPS,)),
            pltpu.SemaphoreType.DMA((GROUPS,)),
            pltpu.SemaphoreType.DMA((GROUPS,)),
            pltpu.SemaphoreType.DMA((GROUPS,)),
            pltpu.SemaphoreType.DMA,
        ],
        compiler_params=pltpu.CompilerParams(vmem_limit_bytes=60 * 1024 * 1024),
        name="attend",
    )(lengths, adapters, holder, gain.reshape(1, D), jnp.asarray(rope_table()), x, proj, adp, wo)


class Route:
    def __init__(self, core, refs):
        self.core = core
        (self.w_hbm, self.adp_hbm, self.adp_out, self.w_v, self.a_send, self.a_recv, self.a_sib, self.w_send, self.w_recv, self.w_sib) = refs
        req = lax.axis_index("req")
        self.x = lax.axis_index("ad")
        self.z = req // (NY * 2)
        self.y = req // 2 % NY
        self.sent = []
        self.events = []

    def device(self, dz=0, dy=0, dx=0, core=None):
        z = (self.z + dz + NZ) % NZ
        y = (self.y + dy + NY) % NY
        core = self.core if core is None else core
        return ((z * NY + y) * 2 + core, (self.x + dx + NX) % NX)

    def adapter_ref(self, oz, oy, core, part, source=False):
        if source and oz == 0 and oy == 0 and core == self.core:
            ref = self.adp_hbm
            return ref if part is None else ref.at[:, pl.ds(part * (APC // 2), APC // 2)]
        owner = (((self.z + oz + NZ) % NZ) * NY + (self.y + oy + NY) % NY) * 2 + core
        if part is None:
            return self.adp_out.at[owner]
        return self.adp_out.at[owner, :, pl.ds(part * (APC // 2), APC // 2)]

    @staticmethod
    def piece(oz, oy, part):
        return (oz % NZ) * NY + oy % NY + (32 if part == 1 else 0)

    def adapter_copy(self, oz, oy, part, dz, dy):
        link = {(1, 0): 0, (-1, 0): 1, (0, 1): 2, (0, -1): 3}[(dz, dy)]
        noz, noy = self.norm(oz - dz, oy - dy)
        ref = self.adapter_ref(oz, oy, self.core, part)
        return pltpu.make_async_remote_copy(
            src_ref=self.adapter_ref(oz, oy, self.core, part, True), dst_ref=ref,
            send_sem=self.a_send.at[link, self.piece(oz, oy, part)], recv_sem=self.a_recv.at[self.piece(noz, noy, part)],
            device_id=self.device(dz, dy), device_id_type=pl.DeviceIdType.MESH,
        )

    @staticmethod
    def norm(oz, oy):
        return (4 if oz == -4 else oz), (2 if oy == -2 else oy)

    def adapter_to_sibling(self, oz, oy, part):
        return pltpu.make_async_remote_copy(
            src_ref=self.adapter_ref(oz, oy, self.core, part, True), dst_ref=self.adapter_ref(oz, oy, self.core, part),
            send_sem=self.a_send.at[4, self.piece(oz, oy, part)], recv_sem=self.a_sib.at[self.piece(oz, oy, part)],
            device_id=self.device(core=1 - self.core), device_id_type=pl.DeviceIdType.MESH,
        )

    def adapter_arrival(self, oz, oy, part):
        ref = self.adapter_ref(oz, oy, self.core, part)
        k = self.piece(oz, oy, part)
        return pltpu.make_async_remote_copy(
            src_ref=ref, dst_ref=ref, send_sem=self.a_send.at[0, k], recv_sem=self.a_recv.at[k],
            device_id=self.device(1, 0), device_id_type=pl.DeviceIdType.MESH,
        )

    def adapter_from_sibling(self, oz, oy, part):
        ref = self.adapter_ref(oz, oy, 1 - self.core, part)
        k = self.piece(oz, oy, part)
        return pltpu.make_async_remote_copy(
            src_ref=ref, dst_ref=ref, send_sem=self.a_send.at[4, k], recv_sem=self.a_sib.at[k],
            device_id=self.device(core=1 - self.core), device_id_type=pl.DeviceIdType.MESH,
        )

    def shard_ref(self, ox, half, sub, source=False):
        rows = pl.ds(sub * SUBR, SUBR)
        if source and ox == 0:
            return self.w_hbm.at[half, rows]
        return self.w_v.at[(self.x + ox + NX) % NX, half, rows]

    @staticmethod
    def shard_piece(ox, sub):
        return {-1: 0, 1: 1, 2: 2, 0: 3}[ox] * SUBS + sub

    def shard_copy(self, ox, sub, dx):
        nox = {-2: 2}.get(ox - dx, ox - dx)
        return pltpu.make_async_remote_copy(
            src_ref=self.shard_ref(ox, self.core, sub, True), dst_ref=self.shard_ref(ox, self.core, sub),
            send_sem=self.w_send.at[0 if dx > 0 else 1, self.shard_piece(ox, sub)], recv_sem=self.w_recv.at[self.shard_piece(nox, sub)],
            device_id=self.device(dx=dx), device_id_type=pl.DeviceIdType.MESH,
        )

    def shard_to_sibling(self, ox, sub, core=None):
        ref = self.shard_ref(ox, self.core if core is None else core, sub)
        k = self.shard_piece(ox, sub)
        return pltpu.make_async_remote_copy(
            src_ref=ref, dst_ref=ref, send_sem=self.w_send.at[2, k], recv_sem=self.w_sib.at[k],
            device_id=self.device(core=1 - self.core), device_id_type=pl.DeviceIdType.MESH,
        )

    def shard_arrival(self, ox, sub):
        ref = self.shard_ref(ox, self.core, sub)
        k = self.shard_piece(ox, sub)
        return pltpu.make_async_remote_copy(
            src_ref=ref, dst_ref=ref, send_sem=self.w_send.at[0, k], recv_sem=self.w_recv.at[k],
            device_id=self.device(dx=1), device_id_type=pl.DeviceIdType.MESH,
        )

    def plan(self):
        ev = self.events
        send = lambda oz, oy, part, dz, dy: (lambda: self.adapter_copy(oz, oy, part, dz, dy))
        sib = lambda oz, oy, part: (lambda: self.adapter_to_sibling(oz, oy, part))
        got = lambda oz, oy, part: (lambda: self.adapter_arrival(oz, oy, part))
        unit = 1.85
        first = []
        for i in range(SUBS):
            first.append(lambda s=i: self.shard_copy(0, s, 1))
            first.append(lambda s=SUBS - 1 - i: self.shard_copy(0, s, -1))
        if self.core == 0:
            start = [send(0, 0, None, 0, 1), send(0, 0, None, 0, -1), send(0, 0, None, 1, 0), send(0, 0, None, -1, 0), sib(0, 0, None)]
            ready = {0: 0.0, -1: 2.5, 1: 2.6, 2: 5.0}
            both = lambda oy: [send(0, oy, None, 1, 0), send(0, oy, None, -1, 0)]
            ev.append((ready[-1], got(0, -1, None), [send(0, -1, 0, 0, 1)] + both(-1) + [sib(0, -1, None)]))
            ev.append((ready[1], got(0, 1, None), [send(0, 1, 1, 0, -1)] + both(1) + [sib(0, 1, None)]))
            ev.append((ready[2], got(0, 2, 0), [sib(0, 2, 0)]))
            ev.append((ready[2] + 0.1, got(0, 2, 1), [sib(0, 2, 1)] + both(2)))
            for dist in (1, 2, 3, 4):
                for n, oy in enumerate((0, -1, 1, 2)):
                    for dz in (1, -1):
                        oz = -dist * dz
                        if dist == 4 and (oy in (0, -1)) != (dz == 1):
                            continue
                        count = 4 * (dist - 1) + n + 1 if dist < 4 else 13 + n % 2
                        t = 3.0 + (2 * unit * count if count < 4 else 4 * unit + unit * count) + (0.1 if dz < 0 else 0.0)
                        sends = []
                        if dist < 3 or (dist == 3 and (oy in (0, -1)) == (dz == 1)):
                            sends.append(send(oz, oy, None, dz, 0))
                        o = 4 if dist == 4 else oz
                        ev.append((t, got(o, oy, None), sends + [sib(o, oy, None)]))
        else:
            start = [send(0, 0, None, 1, 0), send(0, 0, None, -1, 0), send(0, 0, None, 0, 1), send(0, 0, None, 0, -1), sib(0, 0, None)]
            both = lambda oz: [send(oz, 0, None, 0, 1), send(oz, 0, None, 0, -1)]
            for dist in (1, 2, 3):
                for dz in (1, -1):
                    oz = -dist * dz
                    t = 2.0 + 3.0 * dist - 1.5 + (0.1 if dz < 0 else 0.0)
                    nxt = send(oz, 0, None, dz, 0) if dist < 3 else send(oz, 0, 0 if dz == 1 else 1, dz, 0)
                    ev.append((t, got(oz, 0, None), [nxt] + both(oz) + [sib(oz, 0, None)]))
            ev.append((12.0, got(4, 0, 0), [sib(4, 0, 0)]))
            ev.append((12.1, got(4, 0, 1), [sib(4, 0, 1)] + both(4)))
            order = (0, -1, 1, -2, 2, -3, 3, 4)
            for n, oz in enumerate(order):
                for dy in (1, -1):
                    t = 3.0 + 1.9 * n + (0.1 if dy < 0 else 0.0)
                    t = max(t, 14.2 if oz == 4 else 0.0)
                    sends = []
                    if (oz <= 0) == (dy == 1):
                        sends.append(send(oz, -dy, None, 0, dy))
                    ev.append((t, got(oz, -dy, None), sends + [sib(oz, -dy, None)]))
            for n in range(4):
                for oz in ((0, -1, -2, -3)[n], (1, 2, 3, 4)[n]):
                    ev.append((18.5 + 1.9 * n, got(oz, 2, None), [sib(oz, 2, None)]))
        wsib = lambda ox, s: (lambda: self.shard_to_sibling(ox, s))
        for i in range(SUBS):
            t = 2.0 + 6.3 * (i + 1)
            for dx, s in ((1, i), (-1, SUBS - 1 - i)):
                sends = [wsib(-dx, s)]
                if i < SUBS // 2:
                    sends.insert(0, lambda dx=dx, s=s: self.shard_copy(-dx, s, dx))
                ev.append((t, lambda dx=dx, s=s: self.shard_arrival(-dx, s), sends))
        for i in range(SUBS // 2):
            t = 2.0 + 6.3 * (SUBS + i + 1)
            for s in (i, SUBS - 1 - i):
                ev.append((t, lambda s=s: self.shard_arrival(2, s), [wsib(2, s)]))
        ev.sort(key=lambda e: e[0])
        order = {}
        self.start = start[:4] + first + start[4:]

    def emit_start(self):
        for make in self.start:
            make().start()
            self.sent.append(make)

    def emit_until(self, t):
        while self.events and self.events[0][0] < t:
            _, wait, sends = self.events.pop(0)
            wait().wait_recv()
            for make in sends:
                make().start()
                self.sent.append(make)

    def emit_shard_from_sibling(self, ox):
        for s in range(SUBS):
            self.shard_to_sibling(ox, s, 1 - self.core).wait_recv()

    def emit_finish(self):
        for oz in range(-3, 5):
            for oy in (0, -1, 1, 2):
                halves = (oz, oy) == ((4, 0) if self.core == 0 else (0, 2))
                for part in ((0, 1) if halves else (None,)):
                    self.adapter_from_sibling(oz, oy, part).wait_recv()
        for make in self.sent:
            make().wait_send()


def gather_kernel(
    x_hbm, gain_ref, w_hbm, adp_hbm, proj_hbm, adp_out,
    x_v, n_v, w_v, proj_v, adp_v,
    a_send, a_recv, a_sib, w_send, w_recv, w_sib, sem_x, sem_w, sem_a, sem_b, sem_p,
):
    req = lax.axis_index("req")
    x_pos = lax.axis_index("ad")
    core = req % 2
    refs = (w_hbm, adp_hbm, adp_out, w_v, a_send, a_recv, a_sib, w_send, w_recv, w_sib)
    routes = [Route(c, refs) for c in range(2)]
    barrier = pltpu.get_barrier_semaphore()

    def both(f):
        for c in range(2):
            @pl.when(core == c)
            def _(c=c):
                f(routes[c])

    own_x = pltpu.make_async_copy(x_hbm, x_v, sem_x)
    own_x.start()
    own_w = pltpu.make_async_copy(w_hbm, w_v.at[x_pos], sem_w)
    own_w.start()
    own_a = pltpu.make_async_copy(adp_hbm, adp_v, sem_a)
    own_a.start()

    def greet(r):
        near = [r.device(dz=1), r.device(dz=-1), r.device(dy=1), r.device(dy=-1), r.device(dx=1), r.device(dx=-1), r.device(core=1 - r.core)]
        for dev in near:
            pl.semaphore_signal(barrier, inc=1, device_id=dev, device_id_type=pl.DeviceIdType.MESH)

    both(greet)
    pl.semaphore_wait(barrier, 7)

    def begin(r):
        r.plan()
        r.emit_start()

    both(begin)
    own_a.wait()
    keep_a = pltpu.make_async_copy(adp_v, adp_out.at[req], sem_b)
    keep_a.start()
    own_x.wait()

    def norm_rows(i, carry):
        rows = pl.ds(pl.multiple_of(i * 64, 16), 64)
        x = x_v[rows, :].astype(F32)
        inv = lax.rsqrt(jnp.mean(x * x, axis=-1, keepdims=True) + 1e-05)
        n_v[rows, :] = (x * inv * gain_ref[...]).astype(BF16)
        return carry

    lax.fori_loop(0, TOK // 64, norm_rows, 0)
    own_w.wait()

    def project(ox, half, part):
        owner = (x_pos + ox + NX) % NX
        rows = slice(part * 448, part * 448 + 448)
        acc = jnp.dot(n_v[rows, :], w_v[owner, half], preferred_element_type=F32)
        proj_v[owner, rows, half * 384 : half * 384 + 384] = acc.astype(BF16)

    now = 2.5
    outs = []
    for ox in (0, -1, 1, 2):
        if ox:
            now = {-1: 28.3, 1: 31.5, 2: 42.0}[ox]
            both(lambda r: r.emit_until(now))
            both(lambda r: r.emit_shard_from_sibling(ox))
        for half in range(2):
            for part in range(2):
                both(lambda r: r.emit_until(now))
                project(ox, half, part)
                now += 0.87
        owner = (x_pos + ox + NX) % NX
        copy = pltpu.make_async_copy(proj_v.at[owner], proj_hbm.at[owner], sem_p.at[len(outs)])
        copy.start()
        outs.append(copy)
    both(lambda r: r.emit_until(1e9))
    both(lambda r: r.emit_finish())
    keep_a.wait()
    for copy in outs:
        copy.wait()


def gather_call(x, gain, w_own, adp_own):
    vmem = pl.BlockSpec(memory_space=pltpu.VMEM)
    hbm = pl.BlockSpec(memory_space=pl.ANY)
    dma = pltpu.SemaphoreType.DMA
    return pl.pallas_call(
        gather_kernel,
        out_shape=[
            jax.ShapeDtypeStruct((NX, TOK, SHARD), BF16),
            jax.ShapeDtypeStruct((NZ * NY * 2, RANK, APC), BF16),
        ],
        in_specs=[hbm, vmem, hbm, hbm],
        out_specs=[hbm, hbm],
        scratch_shapes=[
            pltpu.VMEM((TOK, D), BF16),
            pltpu.VMEM((TOK, D), BF16),
            pltpu.VMEM((NX, 2, D, 384), BF16),
            pltpu.VMEM((NX, TOK, SHARD), BF16),
            pltpu.VMEM((RANK, APC), BF16),
            dma((5, 64)), dma((64,)), dma((64,)), dma((3, 16)), dma((16,)), dma((16,)),
            dma, dma, dma, dma, dma((4,)),
        ],
        compiler_params=pltpu.CompilerParams(
            vmem_limit_bytes=60 * 1024 * 1024, collective_id=0, has_side_effects=True
        ),
        name="gather",
    )(x, gain.reshape(1, D), w_own, adp_own)


def body(hidden, gain, wqkv, wo, down, up, lengths, adapters, holder):
    w_own = permute_shard(wqkv, lax.axis_index("ad"))
    adp_own = jnp.concatenate([down[0, :RANK], down[0, RANK:], permute_up(up[0])], axis=1)
    proj, adp = gather_call(hidden, gain, w_own, adp_own)
    return attend_call(lengths[0], adapters[0], holder, gain, hidden, proj, adp, wo)


def solution(mesh):
    placed = (
        P(("req", "ad"), None),
        P(),
        P(None, "ad"),
        P(),
        P("req", None, None),
        P("req", None, None),
        P(("req", "ad"), None),
        P(("req", "ad"), None),
        P(),
    )
    return jax.shard_map(
        body, mesh=mesh, in_specs=placed, out_specs=P(("req", "ad"), None), check_vma=False
    )
```

```python
import math

import jax
import jax.numpy as jnp
import ml_dtypes
import numpy as np
from jax import lax
from jax.experimental import pallas as pl
from jax.experimental.pallas import tpu as pltpu
from jax.sharding import PartitionSpec as P

D = 1536
HEADS = 16
KV_HEADS = 8
HEAD_DIM = 96
HALF = 48
PAIR = 28
RANK = 16
SHARD = 768
TOK = 896
GROUPS = 8
GTOK = 112
GREQ = 8
KPAD = 128
UPC = 2304
APC = 2 * D + UPC
NZ, NY, NX = 8, 4, 4
SUBR = D // 4
MESH = pl.DeviceIdType.MESH
ROPE_THETA = 100000.0
F32 = jnp.float32
BF16 = jnp.bfloat16
NT = (((1,), (1,)), ((), ()))
SLOT_WINDOW = [(48 * s // 128, (48 * s + 47) // 128 + 1) for s in range(8)]


def rope_table():
    pos = np.arange(16, dtype=np.float32)[:, None]
    inv = np.exp(np.float32(-math.log(ROPE_THETA) * 2.0) * np.arange(HALF, dtype=np.float32) / np.float32(HEAD_DIM))
    ang = (pos * inv[None, :].astype(np.float32)).astype(np.float64)
    full = np.concatenate([np.tile(np.cos(ang), (1, 8)), np.tile(np.sin(ang), (1, 8))], axis=1).astype(np.float32)
    parts = []
    rest = full
    for _ in range(3):
        piece = rest.astype(ml_dtypes.bfloat16)
        parts.append(piece)
        rest = rest - piece.astype(np.float32)
    return np.concatenate(parts, axis=0)


def token_places(len_ref, g):
    t = lax.broadcasted_iota(jnp.int32, (GTOK, KPAD), 0)
    pair = t // PAIR
    first = jnp.zeros((GTOK, KPAD), jnp.int32)
    for p in range(4):
        first = jnp.where(pair == p, len_ref[g * GREQ + 2 * p], first)
    second = (t - pair * PAIR) >= first
    start = pair * PAIR + jnp.where(second, first, 0)
    return t, start, 2 * pair + second.astype(jnp.int32), lax.broadcasted_iota(jnp.int32, (GTOK, KPAD), 1)


DUE = (
    {
        (0, 0, -1, 0): 11.3, (0, 0, 1, 0): 11.3, (0, -1, 0, 0): 11.3, (0, 1, 0, 0): 11.3, (1, -1, 0, 0): 14.5,
        (1, 1, 2, 0): 14.5, (0, 0, 2, 0): 15.3, (0, 0, 2, 1): 15.3, (0, -1, -1, 0): 17.6, (0, 1, -1, 0): 17.6,
        (0, -1, 1, 0): 20.3, (0, 1, 1, 0): 20.3, (1, -1, 2, 0): 22.2, (1, 1, 0, 0): 22.2, (0, -2, 0, 0): 24.3,
        (0, 2, 0, 0): 24.3, (0, -1, 2, 0): 27.6, (0, 1, 2, 0): 27.6, (2, 0, 0, 0): 29.9, (2, 2, 0, 0): 29.9,
        (0, -2, -1, 0): 30.0, (0, 2, -1, 0): 30.0, (0, -2, 1, 0): 32.2, (0, 2, 1, 0): 32.2, (0, -3, 0, 0): 34.5,
        (0, 3, 0, 0): 34.5, (0, -2, 2, 0): 36.7, (0, 2, 2, 0): 36.7, (1, -1, 1, 0): 37.6, (1, 1, 1, 0): 37.6,
        (0, -3, -1, 0): 39.0, (0, 3, -1, 0): 39.0, (2, -1, 0, 0): 39.3, (2, 1, 0, 0): 39.3, (0, -3, 1, 0): 41.2,
        (0, 3, 1, 0): 41.2, (0, 4, 0, 0): 43.5, (0, 3, 2, 0): 43.5, (1, -1, 3, 0): 45.2, (1, 1, 3, 0): 45.2,
        (0, -3, 2, 0): 45.7, (0, 4, 1, 0): 45.7, (0, 4, -1, 0): 48.0, (0, 4, 2, 0): 48.0,
    },
    {
        (0, 0, -1, 0): 11.3, (0, 0, 1, 0): 11.3, (0, -1, 0, 0): 11.3, (0, 1, 0, 0): 11.3, (1, -1, 0, 0): 14.5,
        (1, 1, 2, 0): 14.5, (0, 0, 2, 0): 16.4, (0, -1, 1, 0): 16.4, (0, -2, 0, 0): 17.6, (0, 2, 0, 0): 17.6,
        (0, -1, -1, 0): 18.8, (0, 1, 1, 0): 18.8, (0, 1, -1, 0): 21.0, (0, -2, 1, 0): 21.6, (1, -1, 2, 0): 22.2,
        (1, 1, 0, 0): 22.2, (0, -2, -1, 0): 23.2, (0, 2, 1, 0): 23.8, (0, -3, 0, 0): 23.8, (0, 3, 0, 0): 23.8,
        (0, 2, -1, 0): 25.5, (0, 1, 2, 0): 26.1, (0, -1, 2, 0): 27.7, (0, 4, 0, 0): 27.8, (0, 4, 0, 1): 27.8,
        (0, 2, 2, 0): 28.3, (2, 0, 0, 0): 29.9, (2, 2, 0, 0): 29.9, (0, -2, 2, 0): 30.0, (0, -3, 1, 0): 30.6,
        (0, -3, -1, 0): 32.8, (0, 3, 1, 0): 34.0, (0, 3, -1, 0): 37.3, (1, -1, 1, 0): 37.6, (1, 1, 1, 0): 37.6,
        (0, 4, 1, 0): 38.5, (0, 4, -1, 0): 40.6, (2, 1, 0, 0): 42.8, (2, -1, 0, 0): 44.4, (0, 3, 2, 0): 45.0,
        (1, -1, 3, 0): 45.2, (1, 1, 3, 0): 45.2, (0, -3, 2, 0): 46.7, (0, 4, 2, 0): 47.2,
    },
)


class Route:
    def __init__(self, core, refs):
        self.core = core
        self.adp_v, self.w_v, self.a_send, self.a_recv, self.a_sib, self.w_send, self.w_recv, self.w_sib = refs
        req = lax.axis_index("req")
        self.x = lax.axis_index("ad")
        self.z = req // (NY * 2)
        self.y = req // 2 % NY
        self.sent = []
        self.events = []

    def device(self, dz=0, dy=0, dx=0, sibling=False):
        z = (self.z + dz + NZ) % NZ
        y = (self.y + dy + NY) % NY
        core = 1 - self.core if sibling else self.core
        return ((z * NY + y) * 2 + core, (self.x + dx + NX) % NX)

    def copy(self, ref, send_sem, recv_sem, device):
        return pltpu.make_async_remote_copy(
            src_ref=ref, dst_ref=ref, send_sem=send_sem, recv_sem=recv_sem, device_id=device, device_id_type=MESH
        )

    def adapter_ref(self, oz, oy, core, part):
        owner = (((self.z + oz + NZ) % NZ) * NY + (self.y + oy + NY) % NY) * 2 + core
        if part is None:
            return self.adp_v.at[owner]
        return self.adp_v.at[owner, :, pl.ds(part * (APC // 2), APC // 2)]

    @staticmethod
    def piece(oz, oy, part):
        return (oz % NZ) * NY + oy % NY + (32 if part == 1 else 0)

    def adapter_copy(self, oz, oy, part, dz, dy):
        link = {(1, 0): 0, (-1, 0): 1, (0, 1): 2, (0, -1): 3}[(dz, dy)]
        return self.copy(
            self.adapter_ref(oz, oy, self.core, part), self.a_send.at[link, self.piece(oz, oy, part)],
            self.a_recv.at[self.piece(oz - dz, oy - dy, part)], self.device(dz, dy),
        )

    def adapter_to_sibling(self, oz, oy, part, core=None):
        k = self.piece(oz, oy, part)
        core = self.core if core is None else core
        return self.copy(self.adapter_ref(oz, oy, core, part), self.a_send.at[4, k], self.a_sib.at[k], self.device(sibling=True))

    def adapter_arrival(self, oz, oy, part):
        k = self.piece(oz, oy, part)
        return self.copy(self.adapter_ref(oz, oy, self.core, part), self.a_send.at[0, k], self.a_recv.at[k], self.device(1))

    def block_ref(self, ox, i, core):
        sub = (self.y + i) % 4
        return self.w_v.at[(self.x + ox + NX) % NX, core, pl.ds(pl.multiple_of(sub * SUBR, 16), SUBR)]

    def block_copy(self, i, dx):
        k = (0 if dx > 0 else 4) + i
        return self.copy(self.block_ref(0, i, self.core), self.w_send.at[0 if dx > 0 else 1, k], self.w_recv.at[k], self.device(dx=dx))

    def block_arrival(self, ox, i):
        k = (0 if ox < 0 else 4) + i
        return self.copy(self.block_ref(ox, i, self.core), self.w_send.at[0, k], self.w_recv.at[k], self.device(dx=1))

    def block_to_sibling(self, ox, i, core=None):
        k = (0 if ox < 0 else 4) + i
        core = self.core if core is None else core
        return self.copy(self.block_ref(ox, i, core), self.w_send.at[2, k], self.w_sib.at[k], self.device(sibling=True))

    def far_ref(self, oy, core, ox=2):
        sub = (self.y + oy + 4) % 4
        return self.w_v.at[(self.x + ox + NX) % NX, core, pl.ds(pl.multiple_of(sub * SUBR, 16), SUBR)]

    def far_forward(self, oy):
        dx = 1 if oy == 0 else -1
        k = 8 + oy
        return self.copy(self.far_ref(oy, self.core, -dx), self.w_send.at[0 if dx > 0 else 1, k], self.w_recv.at[k], self.device(dx=dx))

    def far_copy(self, dy):
        return self.copy(self.far_ref(0, self.core), self.w_send.at[3 if dy > 0 else 4, 8], self.w_recv.at[8 + -dy % 4], self.device(dy=dy))

    def far_arrival(self, oy):
        k = 8 + oy % 4
        return self.copy(self.far_ref(oy, self.core), self.w_send.at[0, k], self.w_recv.at[k], self.device(dx=1))

    def far_to_sibling(self, oy, core=None):
        k = 8 + oy % 4
        core = self.core if core is None else core
        return self.copy(self.far_ref(oy, core), self.w_send.at[2, k], self.w_sib.at[k], self.device(sibling=True))

    def plan(self):
        ev = self.events
        send = lambda *a: (lambda: self.adapter_copy(*a))
        sib = lambda *a: (lambda: self.adapter_to_sibling(*a))
        got = lambda *a: (lambda: self.adapter_arrival(*a))
        due = lambda kind, a, b, part=0: DUE[self.core][(kind, a, b, part)]
        z_both = lambda oz, oy: [send(oz, oy, None, 1, 0), send(oz, oy, None, -1, 0)]
        y_both = lambda oz, oy: [send(oz, oy, None, 0, 1), send(oz, oy, None, 0, -1)]
        if self.core == 0:
            self.start = y_both(0, 0) + z_both(0, 0) + [sib(0, 0, None)]
            ev.append((due(0, 0, -1), got(0, -1, None), [send(0, -1, 0, 0, 1)] + z_both(0, -1) + [sib(0, -1, None)]))
            ev.append((due(0, 0, 1), got(0, 1, None), [send(0, 1, 1, 0, -1)] + z_both(0, 1) + [sib(0, 1, None)]))
            ev.append((due(0, 0, 2), got(0, 2, 0), [sib(0, 2, 0)]))
            ev.append((due(0, 0, 2, 1), got(0, 2, 1), [sib(0, 2, 1)] + z_both(0, 2)))
            for dist in (1, 2, 3, 4):
                for n, oy in enumerate((0, -1, 1, 2)):
                    for dz in (1, -1):
                        oz = -dist * dz
                        if dist == 4 and (oy in (0, -1)) != (dz == 1):
                            continue
                        sends = []
                        if dist < 3 or (dist == 3 and (oy in (0, -1)) == (dz == 1)):
                            sends.append(send(oz, oy, None, dz, 0))
                        ev.append((due(0, 4 if oz == -4 else oz, oy), got(oz, oy, None), sends + [sib(oz, oy, None)]))
        else:
            self.start = z_both(0, 0) + y_both(0, 0) + [sib(0, 0, None)]
            for dist in (1, 2, 3):
                for dz in (1, -1):
                    oz = -dist * dz
                    nxt = send(oz, 0, None, dz, 0) if dist < 3 else send(oz, 0, 0 if dz == 1 else 1, dz, 0)
                    ev.append((due(0, oz, 0), got(oz, 0, None), [nxt] + y_both(oz, 0) + [sib(oz, 0, None)]))
            ev.append((due(0, 4, 0), got(4, 0, 0), [sib(4, 0, 0)]))
            ev.append((due(0, 4, 0, 1), got(4, 0, 1), [sib(4, 0, 1)] + y_both(4, 0)))
            for oz in range(-3, 5):
                for dy in (1, -1):
                    sends = [send(oz, -dy, None, 0, dy)] if (oz <= 0) == (dy == 1) else []
                    ev.append((due(0, oz, -dy), got(oz, -dy, None), sends + [sib(oz, -dy, None)]))
            for oz in range(-3, 5):
                ev.append((due(0, oz, 2), got(oz, 2, None), [sib(oz, 2, None)]))
        for i in range(4):
            for ox in (-1, 1):
                sends = [lambda ox=ox, i=i: self.block_to_sibling(ox, i)]
                if (ox, i) in ((-1, 0), (1, 2)):
                    sends = [lambda i=i: self.far_forward(i)] + [
                        lambda i=i, ox=ox: self.block_copy(i, -ox) for i in (1, 3)
                    ] + sends
                ev.append((due(1, ox, i), lambda ox=ox, i=i: self.block_arrival(ox, i), sends))
        for oy in (0, 2, -1, 1):
            sends = [lambda dy=dy: self.far_copy(dy) for dy in (1, -1)] if oy == 0 else []
            ev.append((due(2, oy, 0), lambda oy=oy: self.far_arrival(oy), sends + [lambda oy=oy: self.far_to_sibling(oy)]))
        ev.sort(key=lambda e: e[0])

    def begin(self, makes):
        for make in makes:
            make().start()
            self.sent.append(make)

    def emit_until(self, t):
        while self.events and self.events[0][0] < t:
            _, wait, sends = self.events.pop(0)
            wait().wait_recv()
            self.begin(sends)

    def block_from_sibling(self, ox, i):
        other = 1 - self.core
        if ox == 2:
            self.far_to_sibling(i, other).wait_recv()
        else:
            self.block_to_sibling(ox, i, other).wait_recv()

    def adapters_from_sibling(self):
        for oz in range(-3, 5):
            for oy in (0, -1, 1, 2):
                halves = (oz, oy) == ((4, 0) if self.core == 0 else (0, 2))
                for part in ((0, 1) if halves else (None,)):
                    self.adapter_to_sibling(oz, oy, part, 1 - self.core).wait_recv()

    def finish(self):
        for make in self.sent:
            make().wait_send()


def gather_kernel(
    len_ref, ada_ref, hold_ref, x_hbm, gain_ref, w_hbm, down_hbm, up_hbm, proj_hbm, delta_hbm,
    x_v, n_v, wraw_v, perm_v, permq_v, upraw_v, adp_v, w_v, proj_v, delta_v, acc_v,
    a_send, a_recv, a_sib, w_send, w_recv, w_sib, sem_x, sem_w, sem_d, sem_u, sem_p, sem_o,
):
    req = lax.axis_index("req")
    x_pos = lax.axis_index("ad")
    core = req % 2
    y_pos = req // 2 % NY
    routes = [Route(c, (adp_v, w_v, a_send, a_recv, a_sib, w_send, w_recv, w_sib)) for c in range(2)]
    barrier = pltpu.get_barrier_semaphore()

    def both(f):
        for c in range(2):
            @pl.when(core == c)
            def _(c=c):
                f(routes[c])

    own = [
        pltpu.make_async_copy(up_hbm.at[0], upraw_v, sem_u),
        pltpu.make_async_copy(down_hbm.at[0, pl.ds(0, RANK)], adp_v.at[req, :, pl.ds(0, D)], sem_d.at[0]),
        pltpu.make_async_copy(down_hbm.at[0, pl.ds(RANK, RANK)], adp_v.at[req, :, pl.ds(D, D)], sem_d.at[1]),
        pltpu.make_async_copy(w_hbm, wraw_v, sem_w),
        pltpu.make_async_copy(x_hbm, x_v, sem_x),
    ]
    for copy in own:
        copy.start()

    def greet(r):
        for dev in (r.device(dz=1), r.device(dz=-1), r.device(dy=1), r.device(dy=-1), r.device(dx=1), r.device(dx=-1), r.device(sibling=True)):
            pl.semaphore_signal(barrier, inc=1, device_id=dev, device_id_type=MESH)
        r.plan()

    both(greet)

    row = lax.broadcasted_iota(jnp.int32, (SHARD, 384), 0)
    for h in range(2):
        dst = lax.broadcasted_iota(jnp.int32, (8, 384), 1) + 384 * h
        slot = (dst - 384 * h) // 48
        feat = h * 48 + dst - 384 * h - slot * 48
        q_src = jnp.where(slot < 4, 2 * slot, 2 * slot - 7) * 96 + feat
        k_src = slot * 96 + feat
        src = jnp.where(x_pos < 2, q_src, jnp.where(x_pos == 2, k_src, dst))
        permq_v[h] = jnp.where(row == q_src[0:1], 1.0, 0.0).astype(BF16)
        perm_v[h] = jnp.where(row == src[0:1], 1.0, 0.0).astype(BF16)
    own[0].wait()
    up_q = jnp.concatenate([upraw_v[:, :SHARD], upraw_v[:, SHARD:D]], axis=0)
    for h in range(2):
        moved = jnp.dot(up_q, permq_v[h], preferred_element_type=F32).astype(BF16)
        for b in range(2):
            base = 2 * D + b * SHARD + h * 384
            adp_v[req, :, base : base + 384] = moved[b * RANK : (b + 1) * RANK]
    adp_v[req, :, 2 * D + D :] = upraw_v[:, D:]
    own[3].wait()

    def permute_block(i, half):
        sub = (y_pos + i) % 4
        rows = pl.ds(pl.multiple_of(sub * SUBR, 16), SUBR)
        w_v[x_pos, half, rows, :] = jnp.dot(wraw_v[rows, :], perm_v[half], preferred_element_type=F32).astype(BF16)

    permute_block(0, core)
    own[1].wait()
    own[2].wait()
    pl.semaphore_wait(barrier, 7)
    both(lambda r: r.begin(r.start))
    permute_block(2, core)
    both(lambda r: r.begin([lambda: r.block_copy(0, 1)]))
    permute_block(1, core)
    both(lambda r: r.begin([lambda: r.block_copy(2, -1), lambda: r.block_copy(2, 1), lambda: r.block_copy(0, -1)]))
    permute_block(3, core)
    for i in range(4):
        both(lambda r: r.emit_until(3.2 + i))
        permute_block(i, 1 - core)
    own[4].wait()

    def norm_rows(i, carry):
        rows = pl.ds(pl.multiple_of(i * 64, 16), 64)
        x = x_v[rows, :].astype(F32)
        inv = lax.rsqrt(jnp.mean(x * x, axis=-1, keepdims=True) + 1e-05)
        n_v[rows, :] = (x * inv * gain_ref[...].reshape(1, D)).astype(BF16)
        return carry

    lax.fori_loop(0, TOK // 64, norm_rows, 0)

    outs = []

    def store_shard(owner):
        copy = pltpu.make_async_copy(proj_v.at[owner], proj_hbm.at[owner], sem_p.at[len(outs)])
        copy.start()
        outs.append(copy)

    def project_own(now):
        for half in range(2):
            for part in range(2):
                both(lambda r: r.emit_until(now))
                rows = slice(part * 448, part * 448 + 448)
                acc = jnp.dot(n_v[rows, :], w_v[x_pos, half], preferred_element_type=F32)
                proj_v[x_pos, rows, half * 384 : half * 384 + 384] = acc.astype(BF16)
                now += 0.9
        store_shard(x_pos)

    def project_block(slot, ox, i, step, now):
        both(lambda r: r.emit_until(now))
        both(lambda r: r.block_from_sibling(ox, i))
        owner = (x_pos + ox + NX) % NX
        sub = (y_pos + i + 4) % 4
        deep = pl.ds(pl.multiple_of(sub * SUBR, 128), SUBR)
        for half in range(2):
            cols = slice(half * 384, half * 384 + 384)
            for part in range(2):
                rows = slice(part * 448, part * 448 + 448)
                acc = jnp.dot(n_v[rows, deep], w_v[owner, half, deep, :], preferred_element_type=F32)
                if step:
                    acc = acc + acc_v[slot, rows, cols]
                if step == 3:
                    proj_v[owner, rows, cols] = acc.astype(BF16)
                else:
                    acc_v[slot, rows, cols] = acc
        if step == 3:
            store_shard(owner)

    def low_rank(g, carry):
        rows = pl.ds(pl.multiple_of(g * GTOK, 16), GTOK)
        _, _, request, lanes = token_places(len_ref, g)
        mine = lanes // RANK == request
        owners = [hold_ref[ada_ref[g * GREQ + j]] for j in range(GREQ)]
        downs = jnp.concatenate(
            [adp_v[o, :, :D] for o in owners] + [adp_v[o, :, D : 2 * D] for o in owners], axis=0
        )
        low = lax.dot_general(n_v[rows, :], downs, NT, preferred_element_type=F32)
        for c in range(3):
            part = low[:, 128:] if c == 2 else low[:, :128]
            ups = jnp.concatenate([adp_v[o, :, 2 * D + c * SHARD : 2 * D + (c + 1) * SHARD] for o in owners], axis=0)
            own_low = jnp.where(mine, part, 0.0).astype(BF16)
            delta_v[rows, c * SHARD : (c + 1) * SHARD] = jnp.dot(own_low, ups, preferred_element_type=F32).astype(BF16)
        return carry

    project_own(7.5)
    for slot, ox, i, step, t in (
        (0, -1, 0, 0, 16.0), (1, 1, 2, 0, 17.2), (0, -1, 2, 1, 23.8), (1, 1, 0, 1, 25.0), (2, 2, 0, 0, 31.8), (2, 2, 2, 1, 33.0),
        (0, -1, 1, 2, 39.4), (1, 1, 1, 2, 40.6), (2, 2, -1, 2, 45.6), (2, 2, 1, 3, 46.4), (0, -1, 3, 3, 47.2), (1, 1, 3, 3, 48.1),
    ):
        project_block(slot, ox, i, step, t)
    both(lambda r: r.emit_until(1e9))
    both(lambda r: r.adapters_from_sibling())
    lax.fori_loop(0, GROUPS, low_rank, 0, unroll=2)
    copy = pltpu.make_async_copy(delta_v, delta_hbm, sem_o)
    copy.start()
    outs.append(copy)
    both(lambda r: r.finish())
    for copy in outs:
        copy.wait()


def gather_call(lengths, adapters, holder, x, gain, w, down, up):
    smem = pl.BlockSpec(memory_space=pltpu.SMEM)
    vmem = pl.BlockSpec(memory_space=pltpu.VMEM)
    hbm = pl.BlockSpec(memory_space=pl.ANY)
    dma = pltpu.SemaphoreType.DMA
    return pl.pallas_call(
        gather_kernel,
        out_shape=[jax.ShapeDtypeStruct((NX, TOK, SHARD), BF16), jax.ShapeDtypeStruct((TOK, UPC), BF16)],
        in_specs=[smem, smem, smem, hbm, vmem, hbm, hbm, hbm],
        out_specs=[hbm, hbm],
        scratch_shapes=[
            pltpu.VMEM((TOK, D), BF16),
            pltpu.VMEM((TOK, D), BF16),
            pltpu.VMEM((D, SHARD), BF16),
            pltpu.VMEM((2, SHARD, 384), BF16),
            pltpu.VMEM((2, SHARD, 384), BF16),
            pltpu.VMEM((RANK, UPC), BF16),
            pltpu.VMEM((NZ * NY * 2, RANK, APC), BF16),
            pltpu.VMEM((NX, 2, D, 384), BF16),
            pltpu.VMEM((NX, TOK, SHARD), BF16),
            pltpu.VMEM((TOK, UPC), BF16),
            pltpu.VMEM((3, TOK, SHARD), F32),
            dma((5, 64)), dma((64,)), dma((64,)), dma((5, 16)), dma((16,)), dma((16,)),
            dma, dma, dma((2,)), dma, dma((4,)), dma,
        ],
        compiler_params=pltpu.CompilerParams(
            vmem_limit_bytes=60 * 1024 * 1024, collective_id=0, has_side_effects=True
        ),
        name="gather",
    )(lengths, adapters, holder, x, gain, w, down, up)


def attend_kernel(
    len_ref, tab_ref, x_hbm, proj_hbm, delta_hbm, wo_hbm, out_ref,
    x_v, proj_v, delta_v, wo_v, att_v, kmask_v, vmask_v, k_v, v_v,
    sem_x, sem_p, sem_d, sem_wo,
):
    def row_copies(g):
        rows = pl.ds(pl.multiple_of(g * GTOK, 16), GTOK)
        return (
            pltpu.make_async_copy(proj_hbm.at[:, rows], proj_v.at[:, rows], sem_p.at[g]),
            pltpu.make_async_copy(delta_hbm.at[rows], delta_v.at[rows], sem_d.at[g]),
        )

    def start_group(g, carry):
        for copy in row_copies(g):
            copy.start()
        return carry

    lax.fori_loop(0, GROUPS, start_group, 0)
    wo_copies = []
    for head in range(HEADS):
        kv, parity = head // 2, head % 2
        dst = (kv // 4) * 768 + parity * 384 + (kv % 4) * 96
        wo_copies.append(pltpu.make_async_copy(wo_hbm.at[pl.ds(head * 96, 96)], wo_v.at[pl.ds(dst, 96)], sem_wo.at[head]))
    x_copy = pltpu.make_async_copy(x_hbm, x_v, sem_x)
    for copy in wo_copies + [x_copy]:
        copy.start()

    lane = lax.broadcasted_iota(jnp.int32, (KPAD, 384), 1)
    for s in range(8):
        kmask_v[s] = jnp.where((lane >= 48 * s) & (lane < 48 * s + 48), 1.0, 0.0).astype(BF16)
    for s in range(4):
        vmask_v[s] = jnp.where((lane >= 96 * s) & (lane < 96 * s + 96), 1.0, 0.0).astype(BF16)
    k_v[pl.ds(GTOK, KPAD - GTOK), :] = jnp.zeros((KPAD - GTOK, 768), BF16)
    v_v[pl.ds(GTOK, KPAD - GTOK), :] = jnp.zeros((KPAD - GTOK, 768), BF16)

    def group(g, carry):
        rows = pl.ds(pl.multiple_of(g * GTOK, 16), GTOK)
        t, start, _, lanes = token_places(len_ref, g)
        bias = jnp.where((lanes >= start) & (lanes <= t), 0.0, -jnp.inf).astype(F32)
        onehot = jnp.where((lanes % 16 == t - start) & (lanes < 48), 1.0, 0.0).astype(BF16)[:, :48]
        rot = jnp.dot(onehot, tab_ref[...], preferred_element_type=F32)
        cosine, sine = rot[:, :384], rot[:, 384:]

        def roped(first_half, second_half):
            return first_half * cosine - second_half * sine, second_half * cosine + first_half * sine

        for copy in row_copies(g):
            copy.wait()
        kf, ks = roped(proj_v[2, rows, :384].astype(F32), proj_v[2, rows, 384:].astype(F32))
        k_v[:GTOK, :384] = kf.astype(BF16)
        k_v[:GTOK, 384:] = ks.astype(BF16)
        v_v[:GTOK, :] = (proj_v[3, rows, :].astype(F32) + delta_v[rows, D:].astype(F32)).astype(BF16)

        scale = 1.0 / math.sqrt(HEAD_DIM)
        for half in range(2):
            base = half * SHARD
            q = proj_v[half, rows, :].astype(F32) + delta_v[rows, base : base + SHARD].astype(F32)
            qf, qs = roped(q[:, :384], q[:, 384:])
            qf2 = jnp.concatenate([qf.astype(BF16), pltpu.roll(qf, 192, 1).astype(BF16)], axis=0)
            qs2 = jnp.concatenate([qs.astype(BF16), pltpu.roll(qs, 192, 1).astype(BF16)], axis=0)
            probs = []
            for s in range(4):
                slot = 4 * half + s
                lo, hi = SLOT_WINDOW[slot]
                cols = slice(128 * lo, 128 * hi)
                mask = kmask_v[slot, :, cols]
                kcat = jnp.concatenate([k_v[:, cols] * mask, k_v[:, 384 + 128 * lo : 384 + 128 * hi] * mask], axis=1)
                qcat = jnp.concatenate([qf2[:, cols], qs2[:, cols]], axis=1)
                scores = lax.dot_general(qcat, kcat, NT, preferred_element_type=F32)
                halves = []
                for b in range(2):
                    sc = scores[b * GTOK : (b + 1) * GTOK] * scale + bias
                    weights = jnp.exp(sc - jnp.max(sc, axis=-1, keepdims=True))
                    halves.append((weights / jnp.sum(weights, axis=-1, keepdims=True)).astype(BF16))
                probs.append(jnp.concatenate(halves, axis=0))
            p4 = jnp.concatenate(probs, axis=1)
            vh = v_v[:, half * 384 : half * 384 + 384]
            vstack = jnp.concatenate([vh * vmask_v[s] for s in range(4)], axis=0)
            att = jnp.dot(p4, vstack, preferred_element_type=F32).astype(BF16)
            even, odd = (att[:GTOK], att[GTOK:]) if half == 0 else (att[GTOK:], att[:GTOK])
            att_v[rows, base : base + 384] = even
            att_v[rows, base + 384 : base + 768] = odd
        return carry

    lax.fori_loop(0, GROUPS, group, 0, unroll=2)
    for copy in wo_copies + [x_copy]:
        copy.wait()

    def out_rows(i, carry):
        rows = pl.ds(pl.multiple_of(i * 448, 16), 448)
        for c in range(3):
            cols = slice(512 * c, 512 * c + 512)
            acc = jnp.dot(att_v[rows, :], wo_v[:, cols], preferred_element_type=F32)
            out_ref[rows, cols] = (x_v[rows, cols].astype(F32) + acc).astype(BF16)
        return carry

    lax.fori_loop(0, 2, out_rows, 0)


def attend_call(lengths, x, proj, delta, wo):
    smem = pl.BlockSpec(memory_space=pltpu.SMEM)
    vmem = pl.BlockSpec(memory_space=pltpu.VMEM)
    hbm = pl.BlockSpec(memory_space=pl.ANY)
    dma = pltpu.SemaphoreType.DMA
    return pl.pallas_call(
        attend_kernel,
        out_shape=jax.ShapeDtypeStruct((TOK, D), BF16),
        in_specs=[smem, vmem, hbm, hbm, hbm, hbm],
        out_specs=vmem,
        scratch_shapes=[
            pltpu.VMEM((TOK, D), BF16),
            pltpu.VMEM((4, TOK, SHARD), BF16),
            pltpu.VMEM((TOK, UPC), BF16),
            pltpu.VMEM((D, D), BF16),
            pltpu.VMEM((TOK, D), BF16),
            pltpu.VMEM((8, KPAD, 384), BF16),
            pltpu.VMEM((4, KPAD, 384), BF16),
            pltpu.VMEM((KPAD, 768), BF16),
            pltpu.VMEM((KPAD, 768), BF16),
            dma, dma((GROUPS,)), dma((GROUPS,)), dma((HEADS,)),
        ],
        compiler_params=pltpu.CompilerParams(vmem_limit_bytes=60 * 1024 * 1024),
        name="attend",
    )(lengths, jnp.asarray(rope_table()), x, proj, delta, wo)


def body(hidden, gain, wqkv, wo, down, up, lengths, adapters, holder):
    proj, delta = gather_call(lengths[0], adapters[0], holder, hidden, gain, wqkv, down, up)
    return attend_call(lengths[0], hidden, proj, delta, wo)


def solution(mesh):
    placed = (
        P(("req", "ad"), None),
        P(),
        P(None, "ad"),
        P(),
        P("req", None, None),
        P("req", None, None),
        P(("req", "ad"), None),
        P(("req", "ad"), None),
        P(),
    )
    return jax.shard_map(
        body, mesh=mesh, in_specs=placed, out_specs=P(("req", "ad"), None), check_vma=False
    )
```

```python
import math

import jax
import jax.numpy as jnp
import ml_dtypes
import numpy as np
from jax import lax
from jax.experimental import pallas as pl
from jax.experimental.pallas import tpu as pltpu
from jax.sharding import PartitionSpec as P

D = 1536
HEADS = 16
KV_HEADS = 8
HEAD_DIM = 96
HALF = 48
PAIR = 28
RANK = 16
SHARD = 768
TOK = 896
GROUPS = 8
GTOK = 112
GREQ = 8
KPAD = 128
UPC = 2304
APC = 2 * D + UPC
NZ, NY, NX = 8, 4, 4
SUBR = D // 4
MESH = pl.DeviceIdType.MESH
ROPE_THETA = 100000.0
F32 = jnp.float32
BF16 = jnp.bfloat16
NT = (((1,), (1,)), ((), ()))
SLOT_WINDOW = [(48 * s // 128, (48 * s + 47) // 128 + 1) for s in range(8)]


def rope_table():
    pos = np.arange(16, dtype=np.float32)[:, None]
    inv = np.exp(np.float32(-math.log(ROPE_THETA) * 2.0) * np.arange(HALF, dtype=np.float32) / np.float32(HEAD_DIM))
    ang = (pos * inv[None, :].astype(np.float32)).astype(np.float64)
    full = np.concatenate([np.tile(np.cos(ang), (1, 8)), np.tile(np.sin(ang), (1, 8))], axis=1).astype(np.float32)
    parts = []
    rest = full
    for _ in range(3):
        piece = rest.astype(ml_dtypes.bfloat16)
        parts.append(piece)
        rest = rest - piece.astype(np.float32)
    return np.concatenate(parts, axis=0)


def token_places(len_ref, g):
    t = lax.broadcasted_iota(jnp.int32, (GTOK, KPAD), 0)
    pair = t // PAIR
    first = jnp.zeros((GTOK, KPAD), jnp.int32)
    for p in range(4):
        first = jnp.where(pair == p, len_ref[g * GREQ + 2 * p], first)
    second = (t - pair * PAIR) >= first
    start = pair * PAIR + jnp.where(second, first, 0)
    return t, start, 2 * pair + second.astype(jnp.int32), lax.broadcasted_iota(jnp.int32, (GTOK, KPAD), 1)


DUE = (
    {
        (0, 0, -1, 0): 11.3, (0, 0, 1, 0): 11.3, (0, -1, 0, 0): 11.3, (0, 1, 0, 0): 11.3, (1, -1, 0, 0): 14.5,
        (1, 1, 2, 0): 14.5, (0, 0, 2, 0): 15.3, (0, 0, 2, 1): 15.3, (0, -1, -1, 0): 17.6, (0, 1, -1, 0): 17.6,
        (0, -1, 1, 0): 20.3, (0, 1, 1, 0): 20.3, (1, -1, 2, 0): 22.2, (1, 1, 0, 0): 22.2, (0, -2, 0, 0): 24.3,
        (0, 2, 0, 0): 24.3, (0, -1, 2, 0): 27.6, (0, 1, 2, 0): 27.6, (2, 0, 0, 0): 29.9, (2, 2, 0, 0): 29.9,
        (0, -2, -1, 0): 30.0, (0, 2, -1, 0): 30.0, (0, -2, 1, 0): 32.2, (0, 2, 1, 0): 32.2, (0, -3, 0, 0): 34.5,
        (0, 3, 0, 0): 34.5, (0, -2, 2, 0): 36.7, (0, 2, 2, 0): 36.7, (1, -1, 1, 0): 37.6, (1, 1, 1, 0): 37.6,
        (0, -3, -1, 0): 39.0, (0, 3, -1, 0): 39.0, (2, -1, 0, 0): 39.3, (2, 1, 0, 0): 39.3, (0, -3, 1, 0): 41.2,
        (0, 3, 1, 0): 41.2, (0, 4, 0, 0): 43.5, (0, 3, 2, 0): 43.5, (1, -1, 3, 0): 45.2, (1, 1, 3, 0): 45.2,
        (0, -3, 2, 0): 45.7, (0, 4, 1, 0): 45.7, (0, 4, -1, 0): 48.0, (0, 4, 2, 0): 48.0,
    },
    {
        (0, 0, -1, 0): 11.3, (0, 0, 1, 0): 11.3, (0, -1, 0, 0): 11.3, (0, 1, 0, 0): 11.3, (1, -1, 0, 0): 14.5,
        (1, 1, 2, 0): 14.5, (0, 0, 2, 0): 16.4, (0, -1, 1, 0): 16.4, (0, -2, 0, 0): 17.6, (0, 2, 0, 0): 17.6,
        (0, -1, -1, 0): 18.8, (0, 1, 1, 0): 18.8, (0, 1, -1, 0): 21.0, (0, -2, 1, 0): 21.6, (1, -1, 2, 0): 22.2,
        (1, 1, 0, 0): 22.2, (0, -2, -1, 0): 23.2, (0, 2, 1, 0): 23.8, (0, -3, 0, 0): 23.8, (0, 3, 0, 0): 23.8,
        (0, 2, -1, 0): 25.5, (0, 1, 2, 0): 26.1, (0, -1, 2, 0): 27.7, (0, 4, 0, 0): 27.8, (0, 4, 0, 1): 27.8,
        (0, 2, 2, 0): 28.3, (2, 0, 0, 0): 29.9, (2, 2, 0, 0): 29.9, (0, -2, 2, 0): 30.0, (0, -3, 1, 0): 30.6,
        (0, -3, -1, 0): 32.8, (0, 3, 1, 0): 34.0, (0, 3, -1, 0): 37.3, (1, -1, 1, 0): 37.6, (1, 1, 1, 0): 37.6,
        (0, 4, 1, 0): 38.5, (0, 4, -1, 0): 40.6, (2, 1, 0, 0): 42.8, (2, -1, 0, 0): 44.4, (0, 3, 2, 0): 45.0,
        (1, -1, 3, 0): 45.2, (1, 1, 3, 0): 45.2, (0, -3, 2, 0): 46.7, (0, 4, 2, 0): 47.2,
    },
)


class Route:
    def __init__(self, core, refs):
        self.core = core
        self.adp_v, self.w_v, self.a_send, self.a_recv, self.a_sib, self.w_send, self.w_recv, self.w_sib = refs
        req = lax.axis_index("req")
        self.x = lax.axis_index("ad")
        self.z = req // (NY * 2)
        self.y = req // 2 % NY
        self.sent = []
        self.events = []

    def device(self, dz=0, dy=0, dx=0, sibling=False):
        z = (self.z + dz + NZ) % NZ
        y = (self.y + dy + NY) % NY
        core = 1 - self.core if sibling else self.core
        return ((z * NY + y) * 2 + core, (self.x + dx + NX) % NX)

    def copy(self, ref, send_sem, recv_sem, device):
        return pltpu.make_async_remote_copy(
            src_ref=ref, dst_ref=ref, send_sem=send_sem, recv_sem=recv_sem, device_id=device, device_id_type=MESH
        )

    def adapter_ref(self, oz, oy, core, part):
        owner = (((self.z + oz + NZ) % NZ) * NY + (self.y + oy + NY) % NY) * 2 + core
        if part is None:
            return self.adp_v.at[owner]
        return self.adp_v.at[owner, :, pl.ds(part * (APC // 2), APC // 2)]

    @staticmethod
    def piece(oz, oy, part):
        return (oz % NZ) * NY + oy % NY + (32 if part == 1 else 0)

    def adapter_copy(self, oz, oy, part, dz, dy):
        link = {(1, 0): 0, (-1, 0): 1, (0, 1): 2, (0, -1): 3}[(dz, dy)]
        return self.copy(
            self.adapter_ref(oz, oy, self.core, part), self.a_send.at[link, self.piece(oz, oy, part)],
            self.a_recv.at[self.piece(oz - dz, oy - dy, part)], self.device(dz, dy),
        )

    def adapter_to_sibling(self, oz, oy, part, core=None):
        k = self.piece(oz, oy, part)
        core = self.core if core is None else core
        return self.copy(self.adapter_ref(oz, oy, core, part), self.a_send.at[4, k], self.a_sib.at[k], self.device(sibling=True))

    def adapter_arrival(self, oz, oy, part):
        k = self.piece(oz, oy, part)
        return self.copy(self.adapter_ref(oz, oy, self.core, part), self.a_send.at[0, k], self.a_recv.at[k], self.device(1))

    def block_ref(self, ox, i, core):
        sub = (self.y + i) % 4
        return self.w_v.at[(self.x + ox + NX) % NX, core, pl.ds(pl.multiple_of(sub * SUBR, 16), SUBR)]

    def block_copy(self, i, dx):
        k = (0 if dx > 0 else 4) + i
        return self.copy(self.block_ref(0, i, self.core), self.w_send.at[0 if dx > 0 else 1, k], self.w_recv.at[k], self.device(dx=dx))

    def block_arrival(self, ox, i):
        k = (0 if ox < 0 else 4) + i
        return self.copy(self.block_ref(ox, i, self.core), self.w_send.at[0, k], self.w_recv.at[k], self.device(dx=1))

    def block_to_sibling(self, ox, i, core=None):
        k = (0 if ox < 0 else 4) + i
        core = self.core if core is None else core
        return self.copy(self.block_ref(ox, i, core), self.w_send.at[2, k], self.w_sib.at[k], self.device(sibling=True))

    def far_ref(self, oy, core, ox=2):
        sub = (self.y + oy + 4) % 4
        return self.w_v.at[(self.x + ox + NX) % NX, core, pl.ds(pl.multiple_of(sub * SUBR, 16), SUBR)]

    def far_forward(self, oy):
        dx = 1 if oy == 0 else -1
        k = 8 + oy
        return self.copy(self.far_ref(oy, self.core, -dx), self.w_send.at[0 if dx > 0 else 1, k], self.w_recv.at[k], self.device(dx=dx))

    def far_copy(self, dy):
        return self.copy(self.far_ref(0, self.core), self.w_send.at[3 if dy > 0 else 4, 8], self.w_recv.at[8 + -dy % 4], self.device(dy=dy))

    def far_arrival(self, oy):
        k = 8 + oy % 4
        return self.copy(self.far_ref(oy, self.core), self.w_send.at[0, k], self.w_recv.at[k], self.device(dx=1))

    def far_to_sibling(self, oy, core=None):
        k = 8 + oy % 4
        core = self.core if core is None else core
        return self.copy(self.far_ref(oy, core), self.w_send.at[2, k], self.w_sib.at[k], self.device(sibling=True))

    def plan(self):
        ev = self.events
        send = lambda *a: (lambda: self.adapter_copy(*a))
        sib = lambda *a: (lambda: self.adapter_to_sibling(*a))
        got = lambda *a: (lambda: self.adapter_arrival(*a))
        due = lambda kind, a, b, part=0: DUE[self.core][(kind, a, b, part)]
        z_both = lambda oz, oy: [send(oz, oy, None, 1, 0), send(oz, oy, None, -1, 0)]
        y_both = lambda oz, oy: [send(oz, oy, None, 0, 1), send(oz, oy, None, 0, -1)]
        if self.core == 0:
            self.start = y_both(0, 0) + z_both(0, 0) + [sib(0, 0, None)]
            ev.append((due(0, 0, -1), got(0, -1, None), [send(0, -1, 0, 0, 1)] + z_both(0, -1) + [sib(0, -1, None)]))
            ev.append((due(0, 0, 1), got(0, 1, None), [send(0, 1, 1, 0, -1)] + z_both(0, 1) + [sib(0, 1, None)]))
            ev.append((due(0, 0, 2), got(0, 2, 0), [sib(0, 2, 0)]))
            ev.append((due(0, 0, 2, 1), got(0, 2, 1), [sib(0, 2, 1)] + z_both(0, 2)))
            for dist in (1, 2, 3, 4):
                for n, oy in enumerate((0, -1, 1, 2)):
                    for dz in (1, -1):
                        oz = -dist * dz
                        if dist == 4 and (oy in (0, -1)) != (dz == 1):
                            continue
                        sends = []
                        if dist < 3 or (dist == 3 and (oy in (0, -1)) == (dz == 1)):
                            sends.append(send(oz, oy, None, dz, 0))
                        ev.append((due(0, 4 if oz == -4 else oz, oy), got(oz, oy, None), sends + [sib(oz, oy, None)]))
        else:
            self.start = z_both(0, 0) + y_both(0, 0) + [sib(0, 0, None)]
            for dist in (1, 2, 3):
                for dz in (1, -1):
                    oz = -dist * dz
                    nxt = send(oz, 0, None, dz, 0) if dist < 3 else send(oz, 0, 0 if dz == 1 else 1, dz, 0)
                    ev.append((due(0, oz, 0), got(oz, 0, None), [nxt] + y_both(oz, 0) + [sib(oz, 0, None)]))
            ev.append((due(0, 4, 0), got(4, 0, 0), [sib(4, 0, 0)]))
            ev.append((due(0, 4, 0, 1), got(4, 0, 1), [sib(4, 0, 1)] + y_both(4, 0)))
            for oz in range(-3, 5):
                for dy in (1, -1):
                    sends = [send(oz, -dy, None, 0, dy)] if (oz <= 0) == (dy == 1) else []
                    ev.append((due(0, oz, -dy), got(oz, -dy, None), sends + [sib(oz, -dy, None)]))
            for oz in range(-3, 5):
                ev.append((due(0, oz, 2), got(oz, 2, None), [sib(oz, 2, None)]))
        for i in range(4):
            for ox in (-1, 1):
                sends = [lambda ox=ox, i=i: self.block_to_sibling(ox, i)]
                if (ox, i) in ((-1, 0), (1, 2)):
                    sends = [lambda i=i: self.far_forward(i)] + [
                        lambda i=i, ox=ox: self.block_copy(i, -ox) for i in (1, 3)
                    ] + sends
                ev.append((due(1, ox, i), lambda ox=ox, i=i: self.block_arrival(ox, i), sends))
        for oy in (0, 2, -1, 1):
            sends = [lambda dy=dy: self.far_copy(dy) for dy in (1, -1)] if oy == 0 else []
            ev.append((due(2, oy, 0), lambda oy=oy: self.far_arrival(oy), sends + [lambda oy=oy: self.far_to_sibling(oy)]))
        ev.sort(key=lambda e: e[0])

    def begin(self, makes):
        for make in makes:
            make().start()
            self.sent.append(make)

    def emit_until(self, t):
        while self.events and self.events[0][0] < t:
            _, wait, sends = self.events.pop(0)
            wait().wait_recv()
            self.begin(sends)

    def block_from_sibling(self, ox, i):
        other = 1 - self.core
        if ox == 2:
            self.far_to_sibling(i, other).wait_recv()
        else:
            self.block_to_sibling(ox, i, other).wait_recv()

    def adapters_from_sibling(self):
        for oz in range(-3, 5):
            for oy in (0, -1, 1, 2):
                halves = (oz, oy) == ((4, 0) if self.core == 0 else (0, 2))
                for part in ((0, 1) if halves else (None,)):
                    self.adapter_to_sibling(oz, oy, part, 1 - self.core).wait_recv()

    def finish(self):
        for make in self.sent:
            make().wait_send()


def gather_kernel(
    len_ref, ada_ref, hold_ref, x_hbm, gain_ref, w_hbm, down_hbm, up_hbm, proj_hbm, delta_hbm,
    x_v, n_v, wraw_v, perm_v, permq_v, upraw_v, adp_v, w_v, proj_v, delta_v, acc_v,
    a_send, a_recv, a_sib, w_send, w_recv, w_sib, sem_x, sem_w, sem_d, sem_u, sem_p, sem_o,
):
    req = lax.axis_index("req")
    x_pos = lax.axis_index("ad")
    core = req % 2
    y_pos = req // 2 % NY
    routes = [Route(c, (adp_v, w_v, a_send, a_recv, a_sib, w_send, w_recv, w_sib)) for c in range(2)]
    barrier = pltpu.get_barrier_semaphore()

    def both(f):
        for c in range(2):
            @pl.when(core == c)
            def _(c=c):
                f(routes[c])

    own = [
        pltpu.make_async_copy(up_hbm.at[0], upraw_v, sem_u),
        pltpu.make_async_copy(down_hbm.at[0, pl.ds(0, RANK)], adp_v.at[req, :, pl.ds(0, D)], sem_d.at[0]),
        pltpu.make_async_copy(down_hbm.at[0, pl.ds(RANK, RANK)], adp_v.at[req, :, pl.ds(D, D)], sem_d.at[1]),
        pltpu.make_async_copy(w_hbm, wraw_v, sem_w),
        pltpu.make_async_copy(x_hbm, x_v, sem_x),
    ]
    for copy in own:
        copy.start()

    def greet(r):
        for dev in (r.device(dz=1), r.device(dz=-1), r.device(dy=1), r.device(dy=-1), r.device(dx=1), r.device(dx=-1), r.device(sibling=True)):
            pl.semaphore_signal(barrier, inc=1, device_id=dev, device_id_type=MESH)
        r.plan()

    both(greet)

    row = lax.broadcasted_iota(jnp.int32, (SHARD, 384), 0)
    sources = []
    for h in range(2):
        dst = lax.broadcasted_iota(jnp.int32, (8, 384), 1)
        slot = dst // 48
        feat = h * 48 + dst - slot * 48
        q_src = jnp.where(slot < 4, 2 * slot, 2 * slot - 7) * 96 + feat
        k_src = slot * 96 + feat
        sources.append(jnp.where(x_pos < 2, q_src, jnp.where(x_pos == 2, k_src, dst + 384 * h)))
        permq_v[h] = jnp.where(row == q_src[0:1], 1.0, 0.0).astype(BF16)
    own[0].wait()
    up_q = jnp.concatenate([upraw_v[:, :SHARD], upraw_v[:, SHARD:D]], axis=0)
    for h in range(2):
        moved = jnp.dot(up_q, permq_v[h], preferred_element_type=F32).astype(BF16)
        for b in range(2):
            base = 2 * D + b * SHARD + h * 384
            adp_v[req, :, base : base + 384] = moved[b * RANK : (b + 1) * RANK]
    adp_v[req, :, 2 * D + D :] = upraw_v[:, D:]
    own[1].wait()
    own[2].wait()
    perm_v[core] = jnp.where(row == jnp.where(core == 0, sources[0], sources[1])[0:1], 1.0, 0.0).astype(BF16)
    pl.semaphore_wait(barrier, 7)
    both(lambda r: r.begin(r.start))
    own[3].wait()

    def permute_block(i, half):
        sub = (y_pos + i) % 4
        rows = pl.ds(pl.multiple_of(sub * SUBR, 16), SUBR)
        w_v[x_pos, half, rows, :] = jnp.dot(wraw_v[rows, :], perm_v[half], preferred_element_type=F32).astype(BF16)

    permute_block(0, core)
    permute_block(2, core)
    both(lambda r: r.begin([lambda: r.block_copy(0, 1)]))
    permute_block(1, core)
    both(lambda r: r.begin([lambda: r.block_copy(2, -1), lambda: r.block_copy(2, 1), lambda: r.block_copy(0, -1)]))
    permute_block(3, core)
    perm_v[1 - core] = jnp.where(row == jnp.where(core == 0, sources[1], sources[0])[0:1], 1.0, 0.0).astype(BF16)
    for i in range(4):
        both(lambda r: r.emit_until(3.2 + i))
        permute_block(i, 1 - core)
    own[4].wait()

    def norm_rows(i, carry):
        rows = pl.ds(pl.multiple_of(i * 64, 16), 64)
        x = x_v[rows, :].astype(F32)
        inv = lax.rsqrt(jnp.mean(x * x, axis=-1, keepdims=True) + 1e-05)
        n_v[rows, :] = (x * inv * gain_ref[...].reshape(1, D)).astype(BF16)
        return carry

    lax.fori_loop(0, TOK // 64, norm_rows, 0)

    outs = []

    def store_shard(owner):
        copy = pltpu.make_async_copy(proj_v.at[owner], proj_hbm.at[owner], sem_p.at[len(outs)])
        copy.start()
        outs.append(copy)

    def project_own(now):
        for half in range(2):
            for part in range(2):
                both(lambda r: r.emit_until(now))
                rows = slice(part * 448, part * 448 + 448)
                acc = jnp.dot(n_v[rows, :], w_v[x_pos, half], preferred_element_type=F32)
                proj_v[x_pos, rows, half * 384 : half * 384 + 384] = acc.astype(BF16)
                now += 0.9
        store_shard(x_pos)

    def project_block(slot, ox, i, step, now):
        both(lambda r: r.emit_until(now))
        both(lambda r: r.block_from_sibling(ox, i))
        owner = (x_pos + ox + NX) % NX
        sub = (y_pos + i + 4) % 4
        deep = pl.ds(pl.multiple_of(sub * SUBR, 128), SUBR)
        for half in range(2):
            cols = slice(half * 384, half * 384 + 384)
            for part in range(2):
                rows = slice(part * 448, part * 448 + 448)
                acc = jnp.dot(n_v[rows, deep], w_v[owner, half, deep, :], preferred_element_type=F32)
                if step:
                    acc = acc + acc_v[slot, rows, cols]
                if step == 3:
                    proj_v[owner, rows, cols] = acc.astype(BF16)
                else:
                    acc_v[slot, rows, cols] = acc
        if step == 3:
            store_shard(owner)

    def delta_copy(g):
        rows = pl.ds(pl.multiple_of(g * GTOK, 16), GTOK)
        return pltpu.make_async_copy(delta_v.at[rows], delta_hbm.at[rows], sem_o.at[g])

    def low_rank(g, carry):
        rows = pl.ds(pl.multiple_of(g * GTOK, 16), GTOK)
        _, _, request, lanes = token_places(len_ref, g)
        mine = lanes // RANK == request
        owners = [hold_ref[ada_ref[g * GREQ + j]] for j in range(GREQ)]
        downs = jnp.concatenate(
            [adp_v[o, :, :D] for o in owners] + [adp_v[o, :, D : 2 * D] for o in owners], axis=0
        )
        low = lax.dot_general(n_v[rows, :], downs, NT, preferred_element_type=F32)
        for c in range(3):
            part = low[:, 128:] if c == 2 else low[:, :128]
            ups = jnp.concatenate([adp_v[o, :, 2 * D + c * SHARD : 2 * D + (c + 1) * SHARD] for o in owners], axis=0)
            own_low = jnp.where(mine, part, 0.0).astype(BF16)
            delta_v[rows, c * SHARD : (c + 1) * SHARD] = jnp.dot(own_low, ups, preferred_element_type=F32).astype(BF16)
        delta_copy(g).start()
        return carry

    project_own(7.5)
    for slot, ox, i, step, t in (
        (0, -1, 0, 0, 16.0), (1, 1, 2, 0, 17.2), (0, -1, 2, 1, 23.8), (1, 1, 0, 1, 25.0), (2, 2, 0, 0, 31.8), (2, 2, 2, 1, 33.0),
        (0, -1, 1, 2, 39.4), (1, 1, 1, 2, 40.6), (2, 2, -1, 2, 45.6), (2, 2, 1, 3, 46.4), (0, -1, 3, 3, 47.2), (1, 1, 3, 3, 48.1),
    ):
        project_block(slot, ox, i, step, t)
    both(lambda r: r.emit_until(1e9))
    both(lambda r: r.adapters_from_sibling())
    lax.fori_loop(0, GROUPS, low_rank, 0, unroll=4)
    both(lambda r: r.finish())
    for copy in outs + [delta_copy(g) for g in range(GROUPS)]:
        copy.wait()


def gather_call(lengths, adapters, holder, x, gain, w, down, up):
    smem = pl.BlockSpec(memory_space=pltpu.SMEM)
    vmem = pl.BlockSpec(memory_space=pltpu.VMEM)
    hbm = pl.BlockSpec(memory_space=pl.ANY)
    dma = pltpu.SemaphoreType.DMA
    return pl.pallas_call(
        gather_kernel,
        out_shape=[jax.ShapeDtypeStruct((NX, TOK, SHARD), BF16), jax.ShapeDtypeStruct((TOK, UPC), BF16)],
        in_specs=[smem, smem, smem, hbm, vmem, hbm, hbm, hbm],
        out_specs=[hbm, hbm],
        scratch_shapes=[
            pltpu.VMEM((TOK, D), BF16),
            pltpu.VMEM((TOK, D), BF16),
            pltpu.VMEM((D, SHARD), BF16),
            pltpu.VMEM((2, SHARD, 384), BF16),
            pltpu.VMEM((2, SHARD, 384), BF16),
            pltpu.VMEM((RANK, UPC), BF16),
            pltpu.VMEM((NZ * NY * 2, RANK, APC), BF16),
            pltpu.VMEM((NX, 2, D, 384), BF16),
            pltpu.VMEM((NX, TOK, SHARD), BF16),
            pltpu.VMEM((TOK, UPC), BF16),
            pltpu.VMEM((3, TOK, SHARD), F32),
            dma((5, 64)), dma((64,)), dma((64,)), dma((5, 16)), dma((16,)), dma((16,)),
            dma, dma, dma((2,)), dma, dma((4,)), dma((GROUPS,)),
        ],
        compiler_params=pltpu.CompilerParams(
            vmem_limit_bytes=60 * 1024 * 1024, collective_id=0, has_side_effects=True
        ),
        name="gather",
    )(lengths, adapters, holder, x, gain, w, down, up)


def attend_kernel(
    len_ref, tab_ref, x_hbm, proj_hbm, delta_hbm, wo_hbm, out_ref,
    x_v, proj_v, delta_v, wo_v, att_v, kmask_v, vmask_v, k_v, v_v,
    sem_x, sem_p, sem_d, sem_wo,
):
    def row_copies(g):
        rows = pl.ds(pl.multiple_of(g * GTOK, 16), GTOK)
        return (
            pltpu.make_async_copy(proj_hbm.at[:, rows], proj_v.at[:, rows], sem_p.at[g]),
            pltpu.make_async_copy(delta_hbm.at[rows], delta_v.at[rows], sem_d.at[g]),
        )

    def start_group(g, carry):
        for copy in row_copies(g):
            copy.start()
        return carry

    lax.fori_loop(0, GROUPS, start_group, 0)
    wo_copies = []
    for head in range(HEADS):
        kv, parity = head // 2, head % 2
        dst = (kv // 4) * 768 + parity * 384 + (kv % 4) * 96
        wo_copies.append(pltpu.make_async_copy(wo_hbm.at[pl.ds(head * 96, 96)], wo_v.at[pl.ds(dst, 96)], sem_wo.at[head]))
    x_copy = pltpu.make_async_copy(x_hbm, x_v, sem_x)
    for copy in wo_copies + [x_copy]:
        copy.start()

    lane = lax.broadcasted_iota(jnp.int32, (KPAD, 384), 1)
    for s in range(8):
        kmask_v[s] = jnp.where((lane >= 48 * s) & (lane < 48 * s + 48), 1.0, 0.0).astype(BF16)
    for s in range(4):
        vmask_v[s] = jnp.where((lane >= 96 * s) & (lane < 96 * s + 96), 1.0, 0.0).astype(BF16)
    k_v[pl.ds(GTOK, KPAD - GTOK), :] = jnp.zeros((KPAD - GTOK, 768), BF16)
    v_v[pl.ds(GTOK, KPAD - GTOK), :] = jnp.zeros((KPAD - GTOK, 768), BF16)

    def group(g, carry):
        rows = pl.ds(pl.multiple_of(g * GTOK, 16), GTOK)
        t, start, _, lanes = token_places(len_ref, g)
        bias = jnp.where((lanes >= start) & (lanes <= t), 0.0, -jnp.inf).astype(F32)
        onehot = jnp.where((lanes % 16 == t - start) & (lanes < 48), 1.0, 0.0).astype(BF16)[:, :48]
        rot = jnp.dot(onehot, tab_ref[...], preferred_element_type=F32)
        cosine, sine = rot[:, :384], rot[:, 384:]

        def roped(first_half, second_half):
            return first_half * cosine - second_half * sine, second_half * cosine + first_half * sine

        for copy in row_copies(g):
            copy.wait()
        kf, ks = roped(proj_v[2, rows, :384].astype(F32), proj_v[2, rows, 384:].astype(F32))
        k_v[:GTOK, :384] = kf.astype(BF16)
        k_v[:GTOK, 384:] = ks.astype(BF16)
        v_v[:GTOK, :] = (proj_v[3, rows, :].astype(F32) + delta_v[rows, D:].astype(F32)).astype(BF16)

        scale = 1.0 / math.sqrt(HEAD_DIM)
        for half in range(2):
            base = half * SHARD
            q = proj_v[half, rows, :].astype(F32) + delta_v[rows, base : base + SHARD].astype(F32)
            qf, qs = roped(q[:, :384], q[:, 384:])
            qf2 = jnp.concatenate([qf.astype(BF16), pltpu.roll(qf, 192, 1).astype(BF16)], axis=0)
            qs2 = jnp.concatenate([qs.astype(BF16), pltpu.roll(qs, 192, 1).astype(BF16)], axis=0)
            probs = []
            for s in range(4):
                slot = 4 * half + s
                lo, hi = SLOT_WINDOW[slot]
                cols = slice(128 * lo, 128 * hi)
                mask = kmask_v[slot, :, cols]
                kcat = jnp.concatenate([k_v[:, cols] * mask, k_v[:, 384 + 128 * lo : 384 + 128 * hi] * mask], axis=1)
                qcat = jnp.concatenate([qf2[:, cols], qs2[:, cols]], axis=1)
                scores = lax.dot_general(qcat, kcat, NT, preferred_element_type=F32)
                halves = []
                for b in range(2):
                    sc = scores[b * GTOK : (b + 1) * GTOK] * scale + bias
                    weights = jnp.exp(sc - jnp.max(sc, axis=-1, keepdims=True))
                    halves.append((weights * (1.0 / jnp.sum(weights, axis=-1, keepdims=True))).astype(BF16))
                probs.append(jnp.concatenate(halves, axis=0))
            p4 = jnp.concatenate(probs, axis=1)
            vh = v_v[:, half * 384 : half * 384 + 384]
            vstack = jnp.concatenate([vh * vmask_v[s] for s in range(4)], axis=0)
            att = jnp.dot(p4, vstack, preferred_element_type=F32).astype(BF16)
            even, odd = (att[:GTOK], att[GTOK:]) if half == 0 else (att[GTOK:], att[:GTOK])
            att_v[rows, base : base + 384] = even
            att_v[rows, base + 384 : base + 768] = odd
        return carry

    lax.fori_loop(0, GROUPS, group, 0, unroll=4)
    for copy in wo_copies + [x_copy]:
        copy.wait()

    def out_rows(i, carry):
        rows = pl.ds(pl.multiple_of(i * 448, 16), 448)
        for c in range(3):
            cols = slice(512 * c, 512 * c + 512)
            acc = jnp.dot(att_v[rows, :], wo_v[:, cols], preferred_element_type=F32)
            out_ref[rows, cols] = (x_v[rows, cols].astype(F32) + acc).astype(BF16)
        return carry

    lax.fori_loop(0, 2, out_rows, 0)


def attend_call(lengths, x, proj, delta, wo):
    smem = pl.BlockSpec(memory_space=pltpu.SMEM)
    vmem = pl.BlockSpec(memory_space=pltpu.VMEM)
    hbm = pl.BlockSpec(memory_space=pl.ANY)
    dma = pltpu.SemaphoreType.DMA
    return pl.pallas_call(
        attend_kernel,
        out_shape=jax.ShapeDtypeStruct((TOK, D), BF16),
        in_specs=[smem, vmem, hbm, hbm, hbm, hbm],
        out_specs=vmem,
        scratch_shapes=[
            pltpu.VMEM((TOK, D), BF16),
            pltpu.VMEM((4, TOK, SHARD), BF16),
            pltpu.VMEM((TOK, UPC), BF16),
            pltpu.VMEM((D, D), BF16),
            pltpu.VMEM((TOK, D), BF16),
            pltpu.VMEM((8, KPAD, 384), BF16),
            pltpu.VMEM((4, KPAD, 384), BF16),
            pltpu.VMEM((KPAD, 768), BF16),
            pltpu.VMEM((KPAD, 768), BF16),
            dma, dma((GROUPS,)), dma((GROUPS,)), dma((HEADS,)),
        ],
        compiler_params=pltpu.CompilerParams(vmem_limit_bytes=60 * 1024 * 1024),
        name="attend",
    )(lengths, jnp.asarray(rope_table()), x, proj, delta, wo)


def body(hidden, gain, wqkv, wo, down, up, lengths, adapters, holder):
    proj, delta = gather_call(lengths[0], adapters[0], holder, hidden, gain, wqkv, down, up)
    return attend_call(lengths[0], hidden, proj, delta, wo)


def solution(mesh):
    placed = (
        P(("req", "ad"), None),
        P(),
        P(None, "ad"),
        P(),
        P("req", None, None),
        P("req", None, None),
        P(("req", "ad"), None),
        P(("req", "ad"), None),
        P(),
    )
    return jax.shard_map(
        body, mesh=mesh, in_specs=placed, out_specs=P(("req", "ad"), None), check_vma=False
    )
```
